32 devices in a mesh: expert: 8 (over z, y), tensor: 4 (over x, core).
Axes of the slice: x: 2, y: 2, z: 4, core: 2. Of those that a mesh axis runs over, the one named last changes fastest.
Arguments:
- block_input: bfloat16 [1576, 768], P('expert'), may hold values from -6.5 to 6.5
- attn_gain: float32 [768], replicated, may hold values from 0.1 to 1.9
- attn_proj: bfloat16 [768, 3, 768], P(None, None, 'tensor'), may hold values from -9.021098 to 9.021098
- attn_merge: bfloat16 [768, 768], P('tensor'), may hold values from -1.75 to 1.75
- mixer_gain: float32 [768], replicated, may hold values from 0.1 to 1.9
- router_weight: bfloat16 [768, 4], replicated, may hold values from -0.21875 to 0.21875
- expert_up: bfloat16 [8, 768, 1536], P('expert', None, 'tensor'), may hold values from -0.21875 to 0.21875
- expert_down: bfloat16 [8, 1536, 768], P('expert', 'tensor'), may hold values from -0.109375 to 0.109375
- routes: int32 [1576, 2], P('expert'), may hold values from 0 to 3, all different within a row; in each aligned block of 197 rows (0 to 196, 197 to 393, ...) at most 192 rows name the same one
- keep_mask: int32 [1576, 2], P('expert'), may hold values 0 or 1
- out_grad: bfloat16 [1576, 768], P('expert'), may hold values from -18.5 to 18.5
Outputs:
- block_output: bfloat16 [1576, 768], P('expert')
- input_grad: float32 [1576, 768], P('expert')
- attn_gain_grad: float32 [768], replicated
- attn_proj_grad: float32 [768, 3, 768], P(None, None, 'tensor')
- attn_merge_grad: float32 [768, 768], P('tensor')
- mixer_gain_grad: float32 [768], replicated
- router_grad: float32 [768, 4], replicated
- expert_up_grad: float32 [8, 768, 1536], P('expert', None, 'tensor')
- expert_down_grad: float32 [8, 1536, 768], P('expert', 'tensor')
The draws below stay inside these ranges and needn't reach their ends.
Inputs may be any that keep to these rules, and one draw needn't show every extreme that they name: `routes`: in each aligned block of 197 rows no expert is named by more than 192 rows, a bound that some block reaches; a row names two different experts.
All inputs are finite; a program needn't handle non-finite values. No bound on the sum of `keep_mask` on one device may be relied on, other than what follows from the above.
Results may differ from the reference program's by a relative error of at most 0.028.
The reference program's roundings to bfloat16 on the way count: a program that leaves them out, or rounds other values in their place, can miss the bound.
Values may be sent and summed in bfloat16 or wider, within the bound.
A program may use at most 128 MiB of HBM per device.

```python
import math
import jax
import jax.numpy as jnp
import numpy as np
from jax import lax

D = 768
FF = 3072
HEADS = 12
SEQ = 197
PAIR = 2
IMG_DEV = 1
HEAD = 64
EXPERTS = 4
TOK_DEV = 197
TOKENS = 1576
CAP = 192
N_EXPERT = 8
N_TENSOR = 4


def draw_block_input(key, part):
    first_key = jax.random.fold_in(key, 0)
    base = jnp.clip(jax.random.normal(first_key, (TOKENS, D), jnp.float32), -6.0, 6.0)
    return base.astype(jnp.bfloat16)


def draw_attn_proj(key, part):
    first_key = jax.random.fold_in(key, 0)
    base = jnp.clip(jax.random.normal(first_key, (D, 3, D), jnp.float32), -6.0, 6.0) * D ** (-0.5)
    return base.astype(jnp.bfloat16)


def draw_out_grad(key, part):
    first_key = jax.random.fold_in(key, 0)
    positions = jnp.arange(TOKENS, dtype=jnp.float32)
    factor = 1.0 + 2.0 * positions / max(TOKENS - 1, 1)
    base = jnp.clip(jax.random.normal(first_key, (TOKENS, D), jnp.float32), -6.0, 6.0)
    return (base * factor[:, None]).astype(jnp.bfloat16)


def with_ends(drawn, stream_key, smallest, high):
    shape = drawn.shape
    spot = [jax.random.randint(jax.random.fold_in(stream_key, axis), (), 0, shape[axis]) for axis in range(len(shape))]
    drawn = drawn.at[tuple(spot)].set(smallest)
    longest = shape.index(max(shape))
    spot[longest] = (spot[longest] + 1) % shape[longest]
    return drawn.at[tuple(spot)].set(high)


def block_levels(own_key, extent, shards, low, largest):
    level, own = 1.0, jax.random.fold_in(own_key, 6)
    for dim, shards_of in shards:
        steps = jnp.exp(jax.random.uniform(jax.random.fold_in(own, dim), (shards_of,), jnp.float32, low / len(shards), largest / len(shards)))
        level = level * jnp.repeat(steps, extent[dim] // shards_of).reshape([-1 if axis == dim else 1 for axis in range(len(extent))])
    return level


def shared_out(rng, own, number, rows, amount, top, limit, slope):
    sequence = jax.random.permutation(rng, amount)
    crowded, common = load_shares(amount, rows * top, limit, slope, True), load_shares(amount, rows * top, limit, slope, False)
    places = jnp.arange(amount)

    def named(lengths, offset_by):
        used = int((lengths > 0).sum())
        fixed = max(1, used // 4)
        passed = fixed + (places - fixed + offset_by * (used - fixed)) % max(1, amount - fixed)
        return jnp.zeros((amount,), jnp.int32).at[sequence[jnp.where(places < fixed, places, passed)]].set(jnp.asarray(lengths, jnp.int32))

    lengths = jnp.where(number % 4 == 0, named(crowded, number // 4), named(common, number - number // 4 - 1))
    mixed = jax.random.permutation(jax.random.fold_in(own, 3), amount)
    source_of, receiver = mixed[0:amount // 2 * 2:2], mixed[1:amount // 2 * 2:2]
    margin = jnp.minimum(lengths[source_of] - 1, limit - lengths[receiver]) // 2
    margin = jnp.where((source_of == sequence[0]) | (receiver == sequence[0]) | (lengths[receiver] == 0), 0, jnp.maximum(margin, 0))
    passed = jax.random.randint(jax.random.fold_in(own, 4), (amount // 2,), 0, 1 << 20) % (margin + 1)
    lengths = lengths.at[source_of].add(-passed).at[receiver].add(passed)
    items = jnp.searchsorted(jnp.cumsum(lengths), jnp.arange(rows * top), side="right").astype(jnp.int32)
    grid = items.reshape(top, rows).T
    grid = grid[jax.random.permutation(jax.random.fold_in(own, 1), rows)]
    offset_by = jax.random.randint(jax.random.fold_in(own, 2), (rows, 1), 0, top)
    return jnp.take_along_axis(grid, (jnp.arange(top)[None, :] + offset_by) % top, axis=1)


def load_shares(amount, total, bound, skew, full):
    weights = [(1 << 20) // math.isqrt(rank ** skew) + 1 for rank in range(1, amount + 1)]
    largest = bound if full else min(bound, max(-(-total // amount), total * weights[0] // sum(weights)))
    least = 1 if total - largest >= amount - 1 else 0
    given, spare = [largest] + [least] * (amount - 1), total - largest - least * (amount - 1)
    while spare > 0:
        free = [i for i in range(1, amount) if given[i] < largest] or [i for i in range(1, amount) if given[i] < bound]
        pool, budget = sum([weights[i] for i in free]), spare
        for i in free:
            extra = min(bound - given[i], max(1, budget * weights[i] // pool), spare)
            given[i] = given[i] + extra
            spare = spare - extra
    return np.array(given)


def centred(stream_key, dims, scale, bound, cuts=(), kind=jnp.bfloat16):
    drawn = scale * jax.random.normal(stream_key, dims, jnp.float32)
    if cuts:
        drawn = drawn * block_levels(stream_key, dims, cuts, -0.22, 0.18)
    return jnp.clip(drawn, -bound, bound).astype(kind)


def setup_inputs(seed: int = 0) -> dict:
    keys = jax.random.split(jax.random.key(seed), 12)
    block_input = draw_block_input(jax.random.fold_in(keys[11], 71), 0)
    attn_gain = jnp.clip(1.0 + 0.18 * jax.random.normal(keys[1], (D,), jnp.float32), 0.1, 1.9)
    attn_proj = draw_attn_proj(jax.random.fold_in(keys[11], 71), 0)
    attn_merge = centred(keys[3], (D, D), (max(4, D // 64)) ** -0.5, 1.75, ((0, 4),))
    mixer_gain = jnp.clip(1.0 + 0.18 * jax.random.normal(keys[4], (D,), jnp.float32), 0.1, 1.9)
    router_weight = centred(keys[5], (D, EXPERTS), D ** -0.5, 0.21875)
    expert_up = centred(keys[6], (EXPERTS * PAIR, D, FF // PAIR), D ** -0.5, 0.21875, ((0, 8), (2, 4)))
    expert_down = centred(keys[7], (EXPERTS * PAIR, FF // PAIR, D), FF ** -0.5, 0.109375, ((0, 8), (1, 4)))
    routes_keys = jax.random.split(jax.random.fold_in(keys[8], 1), TOKENS // TOK_DEV)
    routes_turns = jax.random.permutation(jax.random.fold_in(keys[8], 3), TOKENS // TOK_DEV)
    routes = jax.vmap(lambda own, number: shared_out(jax.random.fold_in(keys[8], 2), own, number, TOK_DEV, EXPERTS, 2, CAP, 2))(routes_keys, routes_turns).reshape((TOKENS, 2))
    keep_mask = with_ends((jax.random.randint(keys[9], (TOKENS, 2), 0, 8) < 7).astype(jnp.int32), jax.random.fold_in(keys[9], 1), 0, 1)
    out_grad = draw_out_grad(jax.random.fold_in(keys[11], 71), 0)
    return {"block_input": block_input, "attn_gain": attn_gain, "attn_proj": attn_proj, "attn_merge": attn_merge, "mixer_gain": mixer_gain, "router_weight": router_weight, "expert_up": expert_up, "expert_down": expert_down, "routes": routes, "keep_mask": keep_mask, "out_grad": out_grad}


EPS = 1e-06
ROOT_HALF = 0.7071067811865476
INV_ROOT_TAU = 0.3989422804014327

def norm_parts(values):
    center = values - lax.optimization_barrier(jnp.mean(values, axis=-1, keepdims=True))
    inverse = lax.rsqrt(lax.optimization_barrier(jnp.mean(center * center, axis=-1, keepdims=True)) + EPS)
    return (center * inverse, inverse)

def norm_back(upstream, normed, inverse, gain):
    scaled = upstream * gain
    return inverse * (scaled - lax.optimization_barrier(jnp.mean(scaled, axis=-1, keepdims=True)) - normed * lax.optimization_barrier(jnp.mean(scaled * normed, axis=-1, keepdims=True)))

def gelu_value(pre_act):
    return 0.5 * pre_act * (1.0 + lax.erf(pre_act * ROOT_HALF))

def gelu_slope(pre_act):
    return 0.5 * (1.0 + lax.erf(pre_act * ROOT_HALF)) + pre_act * jnp.exp(-0.5 * pre_act * pre_act) * INV_ROOT_TAU

def slot_table(routes, keep_mask, experts):
    labels = jnp.arange(experts, dtype=jnp.int32)
    chosen = routes[:, :, None] == labels[None, None, :]
    hits = jnp.where(chosen & (keep_mask[:, :, None] > 0), 1, 0).astype(jnp.int32)
    per_token = lax.optimization_barrier(jnp.sum(hits, axis=1)).astype(jnp.int32)
    before = (jnp.cumsum(per_token, axis=0) - per_token).astype(jnp.int32)
    return lax.optimization_barrier(jnp.sum(jnp.where(chosen, before[:, None, :], 0), axis=2)).astype(jnp.int32)

def attention_forward(block_in, attn_gain, attn_proj, attn_merge):
    wide_in = block_in.astype(jnp.float32)
    normed, inverse = norm_parts(wide_in)
    first_in = (normed * attn_gain).astype(jnp.bfloat16)
    proj = jnp.dot(first_in, attn_proj.reshape(D, 3 * D), preferred_element_type=jnp.float32).astype(jnp.bfloat16)
    head_grid = proj.reshape(IMG_DEV, SEQ, 3, HEADS, HEAD).astype(jnp.float32)
    queries = head_grid[:, :, 0]
    key_heads = head_grid[:, :, 1]
    value_heads = head_grid[:, :, 2]
    raw = jnp.einsum('bqhe,bkhe->bhqk', queries, key_heads) * HEAD ** (-0.5)
    row_top = lax.optimization_barrier(jnp.max(raw, axis=-1))
    log_total = row_top + jnp.log(lax.optimization_barrier(jnp.sum(jnp.exp(raw - row_top[..., None]), axis=-1)))
    attn_probs = jnp.exp(raw - log_total[..., None])
    probs_low = lax.optimization_barrier(attn_probs.astype(jnp.bfloat16)).astype(jnp.float32)
    heads_out = jnp.einsum('bhqk,bkhe->bqhe', probs_low, value_heads).astype(jnp.bfloat16).reshape(TOK_DEV, D)
    middle = wide_in + jnp.dot(heads_out, attn_merge, preferred_element_type=jnp.float32)
    saved = (normed, inverse, first_in, queries, key_heads, value_heads, attn_probs, probs_low, heads_out)
    return (middle, saved)

def reference(block_input, attn_gain, attn_proj, attn_merge, mixer_gain, router_weight, expert_up, expert_down, routes, keep_mask, out_grad):
    blocks = block_input.reshape(N_EXPERT, TOK_DEV, D)
    middle = lax.map(lambda block_in: attention_forward(block_in, attn_gain, attn_proj, attn_merge)[0], blocks).reshape(TOKENS, D)
    normed_two, inverse_two = norm_parts(middle)
    second_in = (normed_two * mixer_gain).astype(jnp.bfloat16)
    logits = jnp.dot(second_in, router_weight, preferred_element_type=jnp.float32)
    labels = jnp.arange(EXPERTS, dtype=jnp.int32)
    first_hot = (routes[:, 0:1] == labels[None, :]).astype(jnp.float32)
    second_hot = (routes[:, 1:2] == labels[None, :]).astype(jnp.float32)
    gate_first = jax.nn.sigmoid(lax.optimization_barrier(jnp.sum(logits * (first_hot - second_hot), axis=1)))
    kept = keep_mask.astype(jnp.float32)
    gate_weights = jnp.stack([gate_first, 1.0 - gate_first], axis=1) * kept
    slots = jax.vmap(lambda route_block, keep_block: slot_table(route_block, keep_block, EXPERTS))(routes.reshape(N_EXPERT, TOK_DEV, 2), keep_mask.reshape(N_EXPERT, TOK_DEV, 2)).reshape(TOKENS, 2)
    device_of = (jnp.arange(TOKENS, dtype=jnp.int32) // TOK_DEV)[:, None]
    span = EXPERTS * N_EXPERT * CAP
    position = (routes * N_EXPERT + device_of) * CAP + slots
    position = jnp.where(keep_mask > 0, position, span).astype(jnp.int32).reshape(-1)
    table = jnp.full((span,), -1, jnp.int32).at[position].set(jnp.arange(TOKENS * 2, dtype=jnp.int32), mode='drop')
    table = table.reshape(EXPERTS, N_EXPERT * CAP)
    grad_wide = out_grad.astype(jnp.float32)
    flat_weights = gate_weights.reshape(-1)
    half_width = FF // PAIR
    quarter = FF // (PAIR * N_TENSOR)
    up_groups = expert_up.reshape(EXPERTS, PAIR, D, half_width)
    down_groups = expert_down.reshape(EXPERTS, PAIR, half_width, D)

    def expert_step(carry, pieces):
        mixed_rows, d_second, gate_dots = carry
        entries, up_part, down_part = pieces
        valid = entries >= 0
        safe = jnp.maximum(entries, 0).astype(jnp.int32)
        owner = (safe // 2).astype(jnp.int32)
        row_block = jnp.where(valid[:, None], second_in[owner].astype(jnp.float32), 0.0)
        row_weight = jnp.where(valid, flat_weights[safe], 0.0)
        up_wide = up_part.astype(jnp.float32)
        down_wide = down_part.astype(jnp.float32)
        pre_act = jnp.einsum('rd,hdf->rhf', row_block, up_wide)
        hidden = lax.optimization_barrier(gelu_value(pre_act).astype(jnp.bfloat16)).astype(jnp.float32)
        rows_count = row_block.shape[0]
        parts = jnp.einsum('rhqf,hqfd->hqrd', hidden.reshape(rows_count, PAIR, N_TENSOR, quarter), down_wide.reshape(PAIR, N_TENSOR, quarter, D)).astype(jnp.bfloat16)
        expert_rows = lax.optimization_barrier(jnp.sum(parts.astype(jnp.float32), axis=(0, 1)))
        mixed_rows = mixed_rows.at[owner].add(row_weight[:, None] * expert_rows)
        grad_rows = grad_wide[owner]
        gate_dots = gate_dots.at[safe].add(jnp.where(valid, lax.optimization_barrier(jnp.sum(grad_rows * expert_rows, axis=1)), 0.0))
        d_rows = lax.optimization_barrier((row_weight[:, None] * grad_rows).astype(jnp.bfloat16)).astype(jnp.float32)
        d_hidden = jnp.einsum('rd,hfd->rhf', d_rows, down_wide)
        down_grad = jnp.einsum('rhf,rd->hfd', hidden, d_rows)
        d_pre = lax.optimization_barrier((d_hidden * gelu_slope(pre_act)).astype(jnp.bfloat16)).astype(jnp.float32)
        up_grad = jnp.einsum('rd,rhf->hdf', row_block, d_pre)
        d_parts = jnp.einsum('rhqf,hdqf->hqrd', d_pre.reshape(rows_count, PAIR, N_TENSOR, quarter), up_wide.reshape(PAIR, D, N_TENSOR, quarter)).astype(jnp.bfloat16)
        d_back = lax.optimization_barrier(jnp.sum(d_parts.astype(jnp.float32), axis=(0, 1)))
        d_second = d_second.at[owner].add(jnp.where(valid[:, None], d_back, 0.0))
        return ((mixed_rows, d_second, gate_dots), (up_grad, down_grad))
    start = (jnp.zeros((TOKENS, D), jnp.float32), jnp.zeros((TOKENS, D), jnp.float32), jnp.zeros((TOKENS * 2,), jnp.float32))
    (moe, d_second, gate_dots), (up_grads, down_grads) = lax.scan(expert_step, start, (table, up_groups, down_groups))
    block_output = (middle + moe).astype(jnp.bfloat16)
    d_gates = gate_dots.reshape(TOKENS, 2) * kept
    d_diff = (d_gates[:, 0] - d_gates[:, 1]) * gate_first * (1.0 - gate_first)
    d_logits = (d_diff[:, None] * (first_hot - second_hot)).astype(jnp.bfloat16)
    router_grad = jnp.dot(second_in.T, d_logits, preferred_element_type=jnp.float32)
    d_second = d_second + jnp.dot(d_logits, router_weight.T, preferred_element_type=jnp.float32)
    mixer_gain_grad = lax.optimization_barrier(jnp.sum(d_second * normed_two, axis=0))
    d_middle = grad_wide + norm_back(d_second, normed_two, inverse_two, mixer_gain)

    def attention_backward(carry, pieces):
        proj_grad, merge_grad, gain_grad = carry
        block_in, d_block = pieces
        unused, saved = attention_forward(block_in, attn_gain, attn_proj, attn_merge)
        normed, inverse, first_in, queries, key_heads, value_heads, attn_probs, probs_low, heads_out = saved
        d_low = d_block.astype(jnp.bfloat16)
        merge_grad = merge_grad + jnp.dot(heads_out.T, d_low, preferred_element_type=jnp.float32)
        d_heads = jnp.dot(d_low, attn_merge.T, preferred_element_type=jnp.float32).astype(jnp.bfloat16)
        d_grid = d_heads.reshape(IMG_DEV, SEQ, HEADS, HEAD).astype(jnp.float32)
        out_grid = heads_out.reshape(IMG_DEV, SEQ, HEADS, HEAD).astype(jnp.float32)
        delta = jnp.einsum('bqhe,bqhe->bhq', d_grid, out_grid)
        d_probs = jnp.einsum('bqhe,bkhe->bhqk', d_grid, value_heads)
        d_raw = (attn_probs * (d_probs - delta[..., None]) * HEAD ** (-0.5)).astype(jnp.bfloat16).astype(jnp.float32)
        d_queries = jnp.einsum('bhqk,bkhe->bqhe', d_raw, key_heads)
        d_keys = jnp.einsum('bhqk,bqhe->bkhe', d_raw, queries)
        d_values = jnp.einsum('bhqk,bqhe->bkhe', probs_low, d_grid)
        d_proj = jnp.stack([d_queries, d_keys, d_values], axis=2).astype(jnp.bfloat16).reshape(TOK_DEV, 3 * D)
        proj_grad = proj_grad + jnp.dot(first_in.T, d_proj, preferred_element_type=jnp.float32)
        d_first = jnp.dot(d_proj, attn_proj.reshape(D, 3 * D).T, preferred_element_type=jnp.float32)
        gain_grad = gain_grad + lax.optimization_barrier(jnp.sum(d_first * normed, axis=0))
        input_block = d_block + norm_back(d_first, normed, inverse, attn_gain)
        return ((proj_grad, merge_grad, gain_grad), input_block)
    start_back = (jnp.zeros((D, 3 * D), jnp.float32), jnp.zeros((D, D), jnp.float32), jnp.zeros((D,), jnp.float32))
    (proj_grad, merge_grad, gain_grad), input_grad = lax.scan(attention_backward, start_back, (blocks, d_middle.reshape(N_EXPERT, TOK_DEV, D)))
    return (block_output, input_grad.reshape(TOKENS, D), gain_grad, proj_grad.reshape(D, 3, D), merge_grad, mixer_gain_grad, router_grad, up_grads.reshape(EXPERTS * PAIR, D, half_width), down_grads.reshape(EXPERTS * PAIR, half_width, D))
```

```python
import functools

import jax
import jax.numpy as jnp
from jax import lax
from jax.experimental import pallas as pl
from jax.experimental.pallas import tpu as pltpu
from jax.sharding import PartitionSpec as P

D = 768
SEQ = 197
PAIR = 2
IMG_DEV = 1
HEAD = 64
TOK_DEV = 197


EPS = 1e-06
ROOT_HALF = 0.7071067811865476
INV_ROOT_TAU = 0.3989422804014327


def norm_parts(values):
    center = values - jnp.mean(values, axis=-1, keepdims=True)
    inverse = lax.rsqrt(jnp.mean(center * center, axis=-1, keepdims=True) + EPS)
    return (center * inverse, inverse)


def norm_back(upstream, normed, inverse, gain):
    scaled = upstream * gain
    return inverse * (
        scaled
        - jnp.mean(scaled, axis=-1, keepdims=True)
        - normed * jnp.mean(scaled * normed, axis=-1, keepdims=True)
    )


def gelu_value(pre_act):
    return 0.5 * pre_act * (1.0 + lax.erf(pre_act * ROOT_HALF))


def gelu_slope(pre_act):
    return (
        0.5 * (1.0 + lax.erf(pre_act * ROOT_HALF))
        + pre_act * jnp.exp(-0.5 * pre_act * pre_act) * INV_ROOT_TAU
    )


def slot_table(routes, keep_mask, experts):
    labels = jnp.arange(experts, dtype=jnp.int32)
    chosen = routes[:, :, None] == labels[None, None, :]
    hits = jnp.where(chosen & (keep_mask[:, :, None] > 0), 1, 0).astype(jnp.int32)
    per_token = jnp.sum(hits, axis=1)
    before = jnp.cumsum(per_token, axis=0) - per_token
    return jnp.sum(jnp.where(chosen, before[:, None, :], 0), axis=2)


def spread_rows(slot_rows, experts, capacity):
    width = slot_rows.shape[-1]
    paired = jnp.broadcast_to(
        slot_rows.reshape(experts, 1, capacity, width), (experts, PAIR, capacity, width)
    )
    paired = paired.reshape(experts * PAIR, capacity, width)
    arrived = lax.all_to_all(paired, "expert", split_axis=0, concat_axis=0, tiled=True)
    return arrived.reshape(-1, width)


def return_rows(partial_terms, experts, capacity):
    width = partial_terms.shape[-1]
    sent_rows = partial_terms.astype(jnp.bfloat16).reshape(experts * PAIR, capacity, width)
    landed = lax.all_to_all(sent_rows, "expert", split_axis=0, concat_axis=0, tiled=True).astype(
        jnp.float32
    )
    return jnp.sum(landed.reshape(experts, PAIR, capacity, width), axis=1).reshape(
        experts * capacity, width
    )


def on_device(
    block_input,
    attn_gain,
    attn_proj,
    attn_merge,
    mixer_gain,
    router_weight,
    expert_up,
    expert_down,
    routes,
    keep_mask,
    out_grad,
):
    experts = lax.axis_size("expert") // PAIR
    capacity = max(8, 4 * TOK_DEV // experts // 8 * 8)
    local_width = attn_proj.shape[2]
    heads_here = local_width // HEAD
    score_scale = HEAD ** (-0.5)
    tokens = block_input.shape[0]
    wide_input = block_input.astype(jnp.float32)
    normed_one, inverse_one = norm_parts(wide_input)
    first_in = (normed_one * attn_gain).astype(jnp.bfloat16)
    proj = jnp.einsum(
        "td,dce->tce", first_in, attn_proj, preferred_element_type=jnp.float32
    ).astype(jnp.bfloat16)
    head_grid = proj.reshape(IMG_DEV, SEQ, 3, heads_here, HEAD)
    queries = head_grid[:, :, 0]
    key_heads = head_grid[:, :, 1]
    value_heads = head_grid[:, :, 2]
    raw = (
        jnp.einsum("bqhe,bkhe->bhqk", queries, key_heads, preferred_element_type=jnp.float32)
        * score_scale
    )
    row_top = jnp.max(raw, axis=-1)
    log_total = row_top + jnp.log(jnp.sum(jnp.exp(raw - row_top[..., None]), axis=-1))
    attn_probs = jnp.exp(raw - log_total[..., None]).astype(jnp.bfloat16)
    heads_out = jnp.einsum(
        "bhqk,bkhe->bqhe", attn_probs, value_heads, preferred_element_type=jnp.float32
    )
    heads_out = heads_out.astype(jnp.bfloat16).reshape(tokens, local_width)
    merge_terms = jnp.dot(heads_out, attn_merge, preferred_element_type=jnp.float32)
    middle = wide_input + lax.psum(merge_terms.astype(jnp.bfloat16), "tensor").astype(jnp.float32)
    normed_two, inverse_two = norm_parts(middle)
    second_in = (normed_two * mixer_gain).astype(jnp.bfloat16)
    logits = jnp.dot(second_in, router_weight, preferred_element_type=jnp.float32)
    labels = jnp.arange(experts, dtype=jnp.int32)
    first_hot = (routes[:, 0:1] == labels[None, :]).astype(jnp.float32)
    second_hot = (routes[:, 1:2] == labels[None, :]).astype(jnp.float32)
    gate_first = jax.nn.sigmoid(jnp.sum(logits * (first_hot - second_hot), axis=1))
    kept = keep_mask.astype(jnp.float32)
    gate_weights = jnp.stack([gate_first, 1.0 - gate_first], axis=1) * kept
    slots = slot_table(routes, keep_mask, experts)
    live_mask = keep_mask > 0
    target = jnp.where(live_mask, routes * capacity + slots, experts * capacity).reshape(-1)
    source = jnp.where(live_mask, routes * capacity + slots, 0)
    send_rows = (
        jnp.zeros((experts * capacity, D), jnp.bfloat16)
        .at[target]
        .set(jnp.repeat(second_in, 2, axis=0), mode="drop")
    )
    arrived = spread_rows(send_rows, experts, capacity)
    pre_act = jnp.dot(arrived, expert_up[0], preferred_element_type=jnp.float32)
    hidden = gelu_value(pre_act).astype(jnp.bfloat16)
    partial_terms = jnp.dot(hidden, expert_down[0], preferred_element_type=jnp.float32)
    expert_rows = return_rows(partial_terms, experts, capacity)
    picked = expert_rows[source] * kept[:, :, None]
    mixed_rows = jnp.sum(gate_weights[:, :, None] * picked, axis=1)
    moe = lax.psum(mixed_rows.astype(jnp.bfloat16), "tensor").astype(jnp.float32)
    block_output = (middle + moe).astype(jnp.bfloat16)
    grad_wide = out_grad.astype(jnp.float32)
    d_rows = (
        (gate_weights[:, :, None] * grad_wide[:, None, :])
        .astype(jnp.bfloat16)
        .reshape(tokens * 2, D)
    )
    d_send = jnp.zeros((experts * capacity, D), jnp.bfloat16).at[target].set(d_rows, mode="drop")
    d_arrived = spread_rows(d_send, experts, capacity)
    d_hidden = lax.dot_general(
        d_arrived, expert_down[0], (((1,), (1,)), ((), ())), preferred_element_type=jnp.float32
    )
    down_local = lax.dot_general(
        hidden, d_arrived, (((0,), (0,)), ((), ())), preferred_element_type=jnp.float32
    )
    d_pre = (d_hidden * gelu_slope(pre_act)).astype(jnp.bfloat16)
    up_local = lax.dot_general(
        arrived, d_pre, (((0,), (0,)), ((), ())), preferred_element_type=jnp.float32
    )
    d_terms = lax.dot_general(
        d_pre, expert_up[0], (((1,), (1,)), ((), ())), preferred_element_type=jnp.float32
    )
    d_back = return_rows(d_terms, experts, capacity)
    d_picked = jnp.sum(d_back[source] * kept[:, :, None], axis=1)
    dots_part = jnp.sum(picked * grad_wide[:, None, :], axis=2)
    d_moe, gate_dots = (
        lax.psum(d_picked.astype(jnp.bfloat16), "tensor").astype(jnp.float32),
        lax.psum(dots_part.astype(jnp.bfloat16), "tensor").astype(jnp.float32),
    )
    d_gates = gate_dots * kept
    d_diff = (d_gates[:, 0] - d_gates[:, 1]) * gate_first * (1.0 - gate_first)
    d_logits = (d_diff[:, None] * (first_hot - second_hot)).astype(jnp.bfloat16)
    router_part = lax.dot_general(
        second_in, d_logits, (((0,), (0,)), ((), ())), preferred_element_type=jnp.float32
    )
    d_second = d_moe + lax.dot_general(
        d_logits, router_weight, (((1,), (1,)), ((), ())), preferred_element_type=jnp.float32
    )
    mixer_part = jnp.sum(d_second * normed_two, axis=0)
    d_middle = grad_wide + norm_back(d_second, normed_two, inverse_two, mixer_gain)
    d_low = d_middle.astype(jnp.bfloat16)
    merge_local = lax.dot_general(
        heads_out, d_low, (((0,), (0,)), ((), ())), preferred_element_type=jnp.float32
    )
    d_heads = lax.dot_general(
        d_low, attn_merge, (((1,), (1,)), ((), ())), preferred_element_type=jnp.float32
    ).astype(jnp.bfloat16)
    d_grid = d_heads.reshape(IMG_DEV, SEQ, heads_here, HEAD)
    out_grid = heads_out.reshape(IMG_DEV, SEQ, heads_here, HEAD)
    delta = jnp.einsum("bqhe,bqhe->bhq", d_grid, out_grid, preferred_element_type=jnp.float32)
    raw_again = (
        jnp.einsum("bqhe,bkhe->bhqk", queries, key_heads, preferred_element_type=jnp.float32)
        * score_scale
    )
    probs_wide = jnp.exp(raw_again - log_total[..., None])
    probs_low = probs_wide.astype(jnp.bfloat16)
    d_probs = jnp.einsum("bqhe,bkhe->bhqk", d_grid, value_heads, preferred_element_type=jnp.float32)
    d_raw = (probs_wide * (d_probs - delta[..., None]) * score_scale).astype(jnp.bfloat16)
    d_queries = jnp.einsum("bhqk,bkhe->bqhe", d_raw, key_heads, preferred_element_type=jnp.float32)
    d_keys = jnp.einsum("bhqk,bqhe->bkhe", d_raw, queries, preferred_element_type=jnp.float32)
    d_values = jnp.einsum("bhqk,bqhe->bkhe", probs_low, d_grid, preferred_element_type=jnp.float32)
    d_proj = (
        jnp.stack([d_queries, d_keys, d_values], axis=2)
        .astype(jnp.bfloat16)
        .reshape(tokens, 3, local_width)
    )
    proj_local = jnp.einsum("td,tce->dce", first_in, d_proj, preferred_element_type=jnp.float32)
    first_terms = jnp.einsum("tce,dce->td", d_proj, attn_proj, preferred_element_type=jnp.float32)
    d_first = lax.psum(first_terms.astype(jnp.bfloat16), "tensor").astype(jnp.float32)
    input_grad = d_middle + norm_back(d_first, normed_one, inverse_one, attn_gain)
    attn_part = jnp.sum(d_first * normed_one, axis=0)
    proj_grad, merge_grad, router_grad, attn_gain_grad, mixer_gain_grad = lax.psum(
        (proj_local, merge_local, router_part, attn_part, mixer_part), "expert"
    )
    return (
        block_output,
        input_grad,
        attn_gain_grad,
        proj_grad,
        merge_grad,
        mixer_gain_grad,
        router_grad,
        up_local[None],
        down_local[None],
    )

MESH = pl.DeviceIdType.MESH
VMEM_LIMIT = 60 * 1024 * 1024


class Net:
    def __init__(self, sizes):
        e = lax.axis_index("expert")
        t = lax.axis_index("tensor")
        self.sizes = sizes
        self.at = [e // sizes[1], e % sizes[1], t // sizes[3], t % sizes[3]]

    def shift(self, rel):
        return [(a + r) % s if r else a for a, r, s in zip(self.at, rel, self.sizes)]

    def ident(self, place):
        return (place[0] * self.sizes[1] + place[1], place[2] * self.sizes[3] + place[3])

    def peers(self, dims):
        found = []
        for d in dims:
            for j in range(1, self.sizes[d]):
                rel = [0, 0, 0, 0]
                rel[d] = j
                found.append(self.ident(self.shift(rel)))
        return found

    def enter(self, dims):
        barrier = pltpu.get_barrier_semaphore()
        near = self.peers(dims)
        for peer in near:
            pl.semaphore_signal(barrier, inc=1, device_id=peer, device_id_type=MESH)
        pl.semaphore_wait(barrier, len(near))


def slot_of(rel, sizes, dims):
    index = 0
    for d in dims:
        index = index * sizes[d] + rel[d] % sizes[d]
    return index


def spread(net, own, out, send, recv, order):
    sizes = net.sizes
    dims = sorted(order)
    sent = []

    def block(rel):
        place = net.shift(rel)
        index = 0
        for d in dims:
            index = index * sizes[d] + place[d]
        return index

    def copy_of(source, rel, d, j):
        there = list(rel)
        there[d] = there[d] - j
        step = [0, 0, 0, 0]
        step[d] = j
        return pltpu.make_async_remote_copy(
            src_ref=source,
            dst_ref=out.at[block(rel)],
            send_sem=send.at[len(sent)],
            recv_sem=recv.at[slot_of(there, sizes, dims)],
            device_id=net.ident(net.shift(step)),
            device_id_type=MESH,
        )

    def forward(source, rel, later):
        for d in later:
            for j in range(1, sizes[d]):
                copy = copy_of(source, rel, d, j)
                copy.start()
                sent.append(copy)

    zero = (0, 0, 0, 0)
    forward(own, zero, order)
    out[block(zero)] = own[...]
    yield
    held = [zero]
    for k, d in enumerate(order):
        fresh = []
        for base in held:
            for j in range(1, sizes[d]):
                rel = list(base)
                rel[d] = j
                here = out.at[block(rel)]
                pltpu.make_async_remote_copy(
                    src_ref=here,
                    dst_ref=here,
                    send_sem=send.at[0],
                    recv_sem=recv.at[slot_of(rel, sizes, dims)],
                    device_id=net.peers([d])[0],
                    device_id_type=MESH,
                ).wait_recv()
                forward(here, rel, order[k + 1 :])
                fresh.append(tuple(rel))
        held = held + fresh
        yield
    for copy in sent:
        copy.wait_send()


def together(steps):
    live = list(steps)
    while live:
        left = []
        for step in live:
            try:
                next(step)
                left.append(step)
            except StopIteration:
                pass
        live = left


def count_of(sizes, order):
    total = 1
    for d in order:
        total *= sizes[d]
    return total


def params(cid):
    return pltpu.CompilerParams(
        collective_id=cid, has_side_effects=True, vmem_limit_bytes=VMEM_LIMIT
    )


def vmem(count):
    return [pl.BlockSpec(memory_space=pltpu.VMEM)] * count


def gather_kernel(sizes, orders, *refs):
    n = len(orders)
    net = Net(sizes)
    net.enter(sorted({d for order in orders for d in order}))
    ins, outs, sems = refs[:n], refs[n : 2 * n], refs[2 * n :]
    together(
        [
            spread(net, ins[i], outs[i], sems[2 * i], sems[2 * i + 1], orders[i])
            for i in range(n)
        ]
    )


def gather_call(sizes, cid, arrays, orders):
    counts = [count_of(sizes, order) for order in orders]
    sems = []
    for count in counts:
        sems += [pltpu.SemaphoreType.DMA((count - 1,)), pltpu.SemaphoreType.DMA((count,))]
    return pl.pallas_call(
        functools.partial(gather_kernel, sizes, orders),
        out_shape=[
            jax.ShapeDtypeStruct((count,) + a.shape, a.dtype) for count, a in zip(counts, arrays)
        ],
        in_specs=vmem(len(arrays)),
        out_specs=vmem(len(arrays)),
        scratch_shapes=sems,
        compiler_params=params(cid),
    )(*arrays)


def scatter_tensor(net, terms, landed, send, recv):
    sizes = net.sizes
    sent = []
    index = 0
    for jx in range(sizes[2]):
        for jc in range(sizes[3]):
            if jx == 0 and jc == 0:
                continue
            place = net.shift((0, 0, jx, jc))
            back = slot_of((0, 0, -jx, -jc), sizes, (2, 3)) - 1
            copy = pltpu.make_async_remote_copy(
                src_ref=terms.at[place[2] * sizes[3] + place[3]],
                dst_ref=landed.at[back],
                send_sem=send.at[index],
                recv_sem=recv.at[back],
                device_id=net.ident(place),
                device_id_type=MESH,
            )
            copy.start()
            sent.append((copy, back))
            index += 1
    return sent


def scatter_finish(net, terms, landed, sent):
    own = net.at[2] * net.sizes[3] + net.at[3]
    total = terms[own].astype(jnp.float32)
    for copy, slot in sent:
        copy.wait()
    for slot in range(len(sent)):
        total = total + landed[slot].astype(jnp.float32)
    return total


def tensor_peers_enter(net, extra):
    barrier = pltpu.get_barrier_semaphore()
    near = []
    for jx in range(net.sizes[2]):
        for jc in range(net.sizes[3]):
            if jx or jc:
                near.append(net.ident(net.shift((0, 0, jx, jc))))
    near = near + net.peers(extra)
    for peer in near:
        pl.semaphore_signal(barrier, inc=1, device_id=peer, device_id_type=MESH)
    pl.semaphore_wait(barrier, len(near))


def merge_kernel(sizes, terms, out, landed, send, recv):
    net = Net(sizes)
    tensor_peers_enter(net, ())
    sent = scatter_tensor(net, terms, landed, send, recv)
    out[...] = scatter_finish(net, terms, landed, sent)


def merge_call(sizes, cid, terms):
    tensor = terms.shape[0]
    return pl.pallas_call(
        functools.partial(merge_kernel, sizes),
        out_shape=jax.ShapeDtypeStruct(terms.shape[1:], jnp.float32),
        in_specs=vmem(1),
        out_specs=pl.BlockSpec(memory_space=pltpu.VMEM),
        scratch_shapes=[
            pltpu.VMEM((tensor - 1,) + terms.shape[1:], terms.dtype),
            pltpu.SemaphoreType.DMA((tensor - 1,)),
            pltpu.SemaphoreType.DMA((tensor - 1,)),
        ],
        compiler_params=params(cid),
    )(terms)


def fold(net, part, out, core_in, core_sum, mid_in, mid_sum, low_in, low_sum, z_in, sems, x_first):
    z, y, x, c = net.at
    depth = net.sizes[0]
    kind = part.dtype
    wide = jnp.float32
    core_peer = net.peers([3])[0]
    first_dim, second_dim = (2, 1) if x_first else (1, 2)
    mid_peer, low_peer = net.peers([first_dim])[0], net.peers([second_dim])[0]
    first_at, second_at = net.at[first_dim], net.at[second_dim]

    def remote(source, target, stage, index, landing, peer):
        return pltpu.make_async_remote_copy(
            src_ref=source,
            dst_ref=target,
            send_sem=sems.at[stage, 0, index],
            recv_sem=sems.at[stage, 1, landing],
            device_id=peer,
            device_id_type=MESH,
        )

    zs = [(z + 1 + k) % depth if k < depth - 1 else z for k in range(depth)]
    core, mid, low, far = [], [], [], []
    for k in range(depth):
        copy = remote(part.at[zs[k], :, :, 1 - c], core_in.at[k], 0, k, k, core_peer)
        copy.start()
        core.append(copy)
    yield
    for k in range(depth):
        core[k].wait_recv()
        core_sum[k] = (part[zs[k], :, :, c].astype(wide) + core_in[k].astype(wide)).astype(kind)
        away = core_sum.at[k, :, 1 - first_at] if x_first else core_sum.at[k, 1 - first_at]
        copy = remote(away, mid_in.at[k], 1, k, k, mid_peer)
        copy.start()
        mid.append(copy)
    yield
    for k in range(depth):
        mid[k].wait_recv()
        near = core_sum[k, :, first_at] if x_first else core_sum[k, first_at]
        mid_sum[k] = (near.astype(wide) + mid_in[k].astype(wide)).astype(kind)
        copy = remote(mid_sum.at[k, 1 - second_at], low_in.at[k], 2, k, k, low_peer)
        copy.start()
        low.append(copy)
    yield
    for k in range(depth):
        low[k].wait_recv()
        total = mid_sum[k, second_at].astype(wide) + low_in[k].astype(wide)
        if k == depth - 1:
            out[...] = total
        else:
            low_sum[k] = total.astype(kind)
            landing = depth - k - 2
            peer = net.ident([zs[k], y, x, c])
            copy = remote(low_sum.at[k], z_in.at[landing], 3, k, landing, peer)
            copy.start()
            far.append(copy)
    yield
    for k in range(depth - 1):
        far[k].wait_recv()
    total = out[...]
    for k in range(depth - 1):
        total = total + z_in[k].astype(wide)
    out[...] = total
    for copy in core + mid + low + far:
        copy.wait_send()


def fold_scratch(sizes, shape, kind):
    depth, ys, xs, cs = sizes
    return [
        pltpu.VMEM((depth, ys, xs) + shape, kind),
        pltpu.VMEM((depth, ys, xs) + shape, kind),
        pltpu.VMEM((depth, 2) + shape, kind),
        pltpu.VMEM((depth, 2) + shape, kind),
        pltpu.VMEM((depth,) + shape, kind),
        pltpu.VMEM((depth - 1,) + shape, kind),
        pltpu.VMEM((depth - 1,) + shape, kind),
        pltpu.SemaphoreType.DMA((4, 2, depth)),
    ]


def fold_kernel(sizes, firsts, *refs):
    n = len(firsts)
    net = Net(sizes)
    net.enter((0, 1, 2, 3))
    ins, outs, rest = refs[:n], refs[n : 2 * n], refs[2 * n :]
    together(
        [
            fold(net, ins[i], outs[i], *rest[8 * i : 8 * i + 8], firsts[i])
            for i in range(n)
        ]
    )


def fold_call(sizes, cid, arrays, firsts):
    shaped = [a.reshape(tuple(sizes) + a.shape[1:]) for a in arrays]
    scratch = []
    for a in arrays:
        scratch += fold_scratch(sizes, a.shape[1:], a.dtype)
    return pl.pallas_call(
        functools.partial(fold_kernel, sizes, firsts),
        out_shape=[jax.ShapeDtypeStruct(a.shape[1:], jnp.float32) for a in arrays],
        in_specs=vmem(len(arrays)),
        out_specs=vmem(len(arrays)),
        scratch_shapes=scratch,
        compiler_params=params(cid),
    )(*shaped)


def tail_kernel(
    sizes,
    gain_row,
    terms,
    d_proj,
    d_low,
    d_middle,
    normed,
    inverse,
    gain,
    small,
    grad_all,
    proj_all,
    low_all,
    small_out,
    landed,
    grad_own,
    small_in,
    small_sum,
    sc_send,
    sc_recv,
    g_send,
    g_recv,
    p_send,
    p_recv,
    l_send,
    l_recv,
    s_send,
    s_recv,
):
    net = Net(sizes)
    tensor_peers_enter(net, (0, 1))
    sent = scatter_tensor(net, terms, landed, sc_send, sc_recv)
    proj_step = spread(net, d_proj, proj_all, p_send, p_recv, (0, 1))
    low_step = spread(net, d_low, low_all, l_send, l_recv, (0, 1, 2, 3))
    next(proj_step)
    next(low_step)
    d_first = scatter_finish(net, terms, landed, sent)
    scaled = d_first * gain[...]
    plain = normed[...]
    mean = jnp.mean(scaled, axis=-1, keepdims=True)
    mixed = jnp.mean(scaled * plain, axis=-1, keepdims=True)
    grad = d_middle[...] + inverse[...] * (scaled - mean - plain * mixed)
    grad_own[...] = grad.astype(jnp.bfloat16)
    grad_step = spread(net, grad_own, grad_all, g_send, g_recv, (2, 3))
    next(grad_step)
    part = jnp.sum(d_first * plain, axis=0, keepdims=True)
    row = lax.broadcasted_iota(jnp.int32, small.shape, 0)
    small_sum[0] = jnp.where(row == gain_row, part, small[...])
    next(proj_step)
    next(low_step)
    stage, index = 0, 0
    rounds = []
    for d in (3, 2, 1, 0):
        copies = []
        for j in range(1, sizes[d]):
            rel = [0, 0, 0, 0]
            rel[d] = j
            landing = index + sizes[d] - 1 - j
            copy = pltpu.make_async_remote_copy(
                src_ref=small_sum.at[stage],
                dst_ref=small_in.at[landing],
                send_sem=s_send.at[index + j - 1],
                recv_sem=s_recv.at[landing],
                device_id=net.ident(net.shift(rel)),
                device_id_type=MESH,
            )
            copy.start()
            copies.append(copy)
        for copy in copies:
            copy.wait_recv()
        total = small_sum[stage]
        for j in range(sizes[d] - 1):
            total = total + small_in[index + j]
        index += sizes[d] - 1
        stage += 1
        if stage < 4:
            small_sum[stage] = total
        else:
            small_out[...] = total
        rounds += copies
        if stage < 3:
            next(low_step)
    for copy in rounds:
        copy.wait_send()
    together([grad_step, low_step, proj_step])


def tail_call(sizes, cid, gain_row, terms, d_proj, d_low, d_middle, normed, inverse, gain, small):
    experts_axis, tensor = sizes[0] * sizes[1], sizes[2] * sizes[3]
    everyone = experts_axis * tensor
    steps = sum(sizes) - 4
    dma = pltpu.SemaphoreType.DMA
    shape = d_low.shape
    return pl.pallas_call(
        functools.partial(tail_kernel, sizes, gain_row),
        out_shape=[
            jax.ShapeDtypeStruct((tensor,) + shape, jnp.bfloat16),
            jax.ShapeDtypeStruct((experts_axis,) + d_proj.shape, jnp.bfloat16),
            jax.ShapeDtypeStruct((everyone,) + shape, jnp.bfloat16),
            jax.ShapeDtypeStruct(small.shape, jnp.float32),
        ],
        in_specs=vmem(8),
        out_specs=vmem(4),
        scratch_shapes=[
            pltpu.VMEM((tensor - 1,) + shape, jnp.bfloat16),
            pltpu.VMEM(shape, jnp.bfloat16),
            pltpu.VMEM((steps,) + small.shape, jnp.float32),
            pltpu.VMEM((4,) + small.shape, jnp.float32),
            dma((tensor - 1,)),
            dma((tensor - 1,)),
            dma((tensor - 1,)),
            dma((tensor,)),
            dma((experts_axis - 1,)),
            dma((experts_axis,)),
            dma((everyone - 1,)),
            dma((everyone,)),
            dma((steps,)),
            dma((steps,)),
        ],
        compiler_params=params(cid),
    )(terms, d_proj, d_low, d_middle, normed, inverse, gain, small)


def on_device_dense(
    sizes,
    block_input,
    attn_gain,
    attn_proj,
    attn_merge,
    mixer_gain,
    router_weight,
    expert_up,
    expert_down,
    routes,
    keep_mask,
    out_grad,
):
    experts_axis, tensor = sizes[0] * sizes[1], sizes[2] * sizes[3]
    experts = experts_axis // PAIR
    tokens = block_input.shape[0]
    rows = -(-(-(-tokens // tensor)) // 8) * 8
    padded = rows * tensor
    local_width = attn_proj.shape[2]
    heads_here = local_width // HEAD
    score_scale = HEAD ** (-0.5)
    start = lax.axis_index("tensor") * rows
    low = jnp.bfloat16
    wide = jnp.float32

    def fill(array):
        return jnp.pad(array, ((0, padded - tokens), (0, 0)))

    def quarter(array):
        return lax.dynamic_slice_in_dim(array, start, rows, axis=0)

    input_q = quarter(fill(block_input)).astype(wide)
    grad_q_low = quarter(fill(out_grad))
    grad_q = grad_q_low.astype(wide)
    route_q = quarter(fill(routes))
    keep_q = quarter(fill(keep_mask))

    normed_one, unused = norm_parts(block_input.astype(wide))
    first_in = (normed_one * attn_gain).astype(low)
    normed_q, inverse_q = norm_parts(input_q)
    first_q = (normed_q * attn_gain).astype(low)
    proj = jnp.einsum("td,dce->tce", first_in, attn_proj, preferred_element_type=wide).astype(low)
    head_grid = proj.reshape(tokens, 3, heads_here, HEAD)
    queries, key_heads, value_heads = head_grid[:, 0], head_grid[:, 1], head_grid[:, 2]
    raw = jnp.einsum("qhe,khe->hqk", queries, key_heads, preferred_element_type=wide) * score_scale
    row_top = jnp.max(raw, axis=-1, keepdims=True)
    powers = jnp.exp(raw - row_top)
    probs_wide = powers / jnp.sum(powers, axis=-1, keepdims=True)
    probs_low = probs_wide.astype(low)
    heads_out = jnp.einsum("hqk,khe->qhe", probs_low, value_heads, preferred_element_type=wide)
    heads_out = heads_out.astype(low).reshape(tokens, local_width)
    merge_terms = jnp.dot(fill(heads_out), attn_merge, preferred_element_type=wide).astype(low)

    merged = merge_call(sizes, 1, merge_terms.reshape(tensor, rows, D))
    middle = input_q + merged
    normed_two, inverse_two = norm_parts(middle)
    second_q = (normed_two * mixer_gain).astype(low)

    codes = jnp.concatenate([route_q, keep_q], axis=1).astype(wide).T
    codes = jnp.pad(codes, ((0, 4), (0, -rows % 128)))
    everywhere = (0, 1, 2, 3)
    second_all, grad_all, first_all, heads_all, codes_all = gather_call(
        sizes,
        2,
        [second_q, grad_q_low, first_q, fill(heads_out), codes],
        [everywhere, (2, 0, 1, 3), (2, 0, 1, 3), (0, 1), everywhere],
    )
    total = experts_axis * padded
    arrived = second_all.reshape(total, D)
    grads = grad_all.reshape(total, D)

    label = lax.axis_index("expert") // PAIR
    code = codes_all[:, :4, :rows].transpose(0, 2, 1).reshape(total, 4)
    labels = jnp.arange(experts, dtype=wide)
    pick_all = (code[:, 0:1] == labels).astype(wide) - (code[:, 1:2] == labels).astype(wide)
    logits_all = jnp.dot(arrived, router_weight, preferred_element_type=wide)
    gate_all = jax.nn.sigmoid(jnp.sum(logits_all * pick_all, axis=1, keepdims=True))
    live_first = jnp.where(code[:, 0:1] == label.astype(wide), code[:, 2:3], 0.0)
    live_second = jnp.where(code[:, 1:2] == label.astype(wide), code[:, 3:4], 0.0)
    weight = live_first * gate_all + live_second * (1.0 - gate_all)
    side = live_first - live_second

    up, down = expert_up[0], expert_down[0]
    pre_act = jnp.dot(arrived, up, preferred_element_type=wide)
    hidden = gelu_value(pre_act).astype(low)
    partial_terms = jnp.dot(hidden, down, preferred_element_type=wide)
    moe_terms = (weight * partial_terms).astype(low)
    dots = jnp.sum(
        (partial_terms * grads.astype(wide)).reshape(experts_axis * tensor, rows, D), axis=2
    ) * side.reshape(experts_axis * tensor, rows)
    dots = jnp.broadcast_to(
        jnp.pad(dots, ((0, 0), (0, -rows % 128)))[:, None, :],
        (experts_axis * tensor, 8, -(-rows // 128) * 128),
    )
    d_rows = (weight * grads.astype(wide)).astype(low)
    d_hidden = lax.dot_general(d_rows, down, (((1,), (1,)), ((), ())), preferred_element_type=wide)
    down_local = lax.dot_general(
        hidden, d_rows, (((0,), (0,)), ((), ())), preferred_element_type=wide
    )
    d_pre = (d_hidden * gelu_slope(pre_act)).astype(low)
    up_local = lax.dot_general(arrived, d_pre, (((0,), (0,)), ((), ())), preferred_element_type=wide)
    d_terms = lax.dot_general(
        d_pre, up, (((1,), (1,)), ((), ())), preferred_element_type=wide
    ).astype(low)

    shape = (experts_axis * tensor, rows, D)
    moe, d_moe, dots_sum = fold_call(
        sizes,
        3,
        [moe_terms.reshape(shape), d_terms.reshape(shape), dots],
        (True, False, True),
    )
    block_q = (middle + moe).astype(low)
    mine = jnp.arange(experts, dtype=jnp.int32)
    pick = (route_q[:, 0:1] == mine).astype(wide) - (route_q[:, 1:2] == mine).astype(wide)
    logits = jnp.dot(second_q, router_weight, preferred_element_type=wide)
    gate_first = jax.nn.sigmoid(jnp.sum(logits * pick, axis=1))
    d_diff = dots_sum[0, :rows] * gate_first * (1.0 - gate_first)
    d_logits = (d_diff[:, None] * pick).astype(low)
    router_part = lax.dot_general(
        d_logits, second_q, (((0,), (0,)), ((), ())), preferred_element_type=wide
    )
    d_second = d_moe + lax.dot_general(
        d_logits, router_weight, (((1,), (1,)), ((), ())), preferred_element_type=wide
    )
    mixer_part = jnp.sum(d_second * normed_two, axis=0, keepdims=True)
    d_middle = grad_q + norm_back(d_second, normed_two, inverse_two, mixer_gain)
    d_low_q = d_middle.astype(low)

    low_rows, block_rows = gather_call(sizes, 4, [d_low_q, block_q], [(2, 3), (2, 3)])
    d_low = low_rows.reshape(padded, D)[:tokens]
    block_output = block_rows.reshape(padded, D)[:tokens]

    d_heads = lax.dot_general(
        d_low, attn_merge, (((1,), (1,)), ((), ())), preferred_element_type=wide
    ).astype(low)
    d_grid = d_heads.reshape(tokens, heads_here, HEAD)
    out_grid = heads_out.reshape(tokens, heads_here, HEAD)
    delta = jnp.sum(d_grid.astype(wide) * out_grid.astype(wide), axis=2).T
    d_probs = jnp.einsum("qhe,khe->hqk", d_grid, value_heads, preferred_element_type=wide)
    d_raw = (probs_wide * (d_probs - delta[..., None]) * score_scale).astype(low)
    d_queries = jnp.einsum("hqk,khe->qhe", d_raw, key_heads, preferred_element_type=wide)
    d_keys = jnp.einsum("hqk,qhe->khe", d_raw, queries, preferred_element_type=wide)
    d_values = jnp.einsum("hqk,qhe->khe", probs_low, d_grid, preferred_element_type=wide)
    d_proj = jnp.concatenate(
        [part.astype(low).reshape(tokens, local_width) for part in (d_queries, d_keys, d_values)],
        axis=1,
    )
    d_proj = fill(d_proj)
    flat_proj = attn_proj.reshape(D, 3 * local_width)
    first_terms = lax.dot_general(
        d_proj, flat_proj, (((1,), (1,)), ((), ())), preferred_element_type=wide
    ).astype(low)
    small = jnp.concatenate([router_part, mixer_part], axis=0)
    small = jnp.pad(small, ((0, 1 + -(experts + 2) % 8), (0, 0)))
    grad_rows, proj_all, low_all, small_all = tail_call(
        sizes,
        5,
        experts + 1,
        first_terms.reshape(tensor, rows, D),
        d_proj,
        d_low_q,
        d_middle,
        normed_q,
        inverse_q,
        attn_gain[None, :],
        small,
    )
    input_grad = grad_rows.reshape(padded, D)[:tokens].astype(wide)
    proj_grad = lax.dot_general(
        first_all.reshape(total, D),
        proj_all.reshape(total, 3 * local_width),
        (((0,), (0,)), ((), ())),
        preferred_element_type=wide,
    ).reshape(D, 3, local_width)
    merge_grad = lax.dot_general(
        heads_all.reshape(total, local_width),
        low_all.reshape(total, D),
        (((0,), (0,)), ((), ())),
        preferred_element_type=wide,
    )
    return (
        block_output,
        input_grad,
        small_all[experts + 1],
        proj_grad,
        merge_grad,
        small_all[experts],
        small_all[:experts].T,
        up_local[None],
        down_local[None],
    )


def program_of(mesh):
    experts_axis, tensor = mesh.shape["expert"], mesh.shape["tensor"]
    if tensor != 4 or experts_axis % 2 or experts_axis < 4:
        return on_device
    capacity = max(8, 4 * TOK_DEV // (experts_axis // PAIR) // 8 * 8)
    rows = -(-(-(-TOK_DEV // tensor)) // 8) * 8
    if 4 * rows * tensor > 5 * capacity:
        return on_device
    return functools.partial(on_device_dense, (experts_axis // 2, 2, tensor // 2, 2))


def solution(mesh):
    in_specs = (
        P("expert", None),
        P(),
        P(None, None, "tensor"),
        P("tensor", None),
        P(),
        P(),
        P("expert", None, "tensor"),
        P("expert", "tensor", None),
        P("expert", None),
        P("expert", None),
        P("expert", None),
    )
    out_specs = (
        P("expert", None),
        P("expert", None),
        P(),
        P(None, None, "tensor"),
        P("tensor", None),
        P(),
        P(),
        P("expert", None, "tensor"),
        P("expert", "tensor", None),
    )
    return jax.shard_map(
        program_of(mesh), mesh=mesh, in_specs=in_specs, out_specs=out_specs, check_vma=False
    )
```

```python
import functools

import jax
import jax.numpy as jnp
from jax import lax
from jax.experimental import pallas as pl
from jax.experimental.pallas import tpu as pltpu
from jax.sharding import PartitionSpec as P

D = 768
SEQ = 197
PAIR = 2
IMG_DEV = 1
HEAD = 64
TOK_DEV = 197


EPS = 1e-06
ROOT_HALF = 0.7071067811865476
INV_ROOT_TAU = 0.3989422804014327


def norm_parts(values):
    center = values - jnp.mean(values, axis=-1, keepdims=True)
    inverse = lax.rsqrt(jnp.mean(center * center, axis=-1, keepdims=True) + EPS)
    return (center * inverse, inverse)


def norm_back(upstream, normed, inverse, gain):
    scaled = upstream * gain
    return inverse * (
        scaled
        - jnp.mean(scaled, axis=-1, keepdims=True)
        - normed * jnp.mean(scaled * normed, axis=-1, keepdims=True)
    )


def gelu_value(pre_act):
    return 0.5 * pre_act * (1.0 + lax.erf(pre_act * ROOT_HALF))


def gelu_slope(pre_act):
    return (
        0.5 * (1.0 + lax.erf(pre_act * ROOT_HALF))
        + pre_act * jnp.exp(-0.5 * pre_act * pre_act) * INV_ROOT_TAU
    )


def slot_table(routes, keep_mask, experts):
    labels = jnp.arange(experts, dtype=jnp.int32)
    chosen = routes[:, :, None] == labels[None, None, :]
    hits = jnp.where(chosen & (keep_mask[:, :, None] > 0), 1, 0).astype(jnp.int32)
    per_token = jnp.sum(hits, axis=1)
    before = jnp.cumsum(per_token, axis=0) - per_token
    return jnp.sum(jnp.where(chosen, before[:, None, :], 0), axis=2)


def spread_rows(slot_rows, experts, capacity):
    width = slot_rows.shape[-1]
    paired = jnp.broadcast_to(
        slot_rows.reshape(experts, 1, capacity, width), (experts, PAIR, capacity, width)
    )
    paired = paired.reshape(experts * PAIR, capacity, width)
    arrived = lax.all_to_all(paired, "expert", split_axis=0, concat_axis=0, tiled=True)
    return arrived.reshape(-1, width)


def return_rows(partial_terms, experts, capacity):
    width = partial_terms.shape[-1]
    sent_rows = partial_terms.astype(jnp.bfloat16).reshape(experts * PAIR, capacity, width)
    landed = lax.all_to_all(sent_rows, "expert", split_axis=0, concat_axis=0, tiled=True).astype(
        jnp.float32
    )
    return jnp.sum(landed.reshape(experts, PAIR, capacity, width), axis=1).reshape(
        experts * capacity, width
    )


def on_device(
    block_input,
    attn_gain,
    attn_proj,
    attn_merge,
    mixer_gain,
    router_weight,
    expert_up,
    expert_down,
    routes,
    keep_mask,
    out_grad,
):
    experts = lax.axis_size("expert") // PAIR
    capacity = max(8, 4 * TOK_DEV // experts // 8 * 8)
    local_width = attn_proj.shape[2]
    heads_here = local_width // HEAD
    score_scale = HEAD ** (-0.5)
    tokens = block_input.shape[0]
    wide_input = block_input.astype(jnp.float32)
    normed_one, inverse_one = norm_parts(wide_input)
    first_in = (normed_one * attn_gain).astype(jnp.bfloat16)
    proj = jnp.einsum(
        "td,dce->tce", first_in, attn_proj, preferred_element_type=jnp.float32
    ).astype(jnp.bfloat16)
    head_grid = proj.reshape(IMG_DEV, SEQ, 3, heads_here, HEAD)
    queries = head_grid[:, :, 0]
    key_heads = head_grid[:, :, 1]
    value_heads = head_grid[:, :, 2]
    raw = (
        jnp.einsum("bqhe,bkhe->bhqk", queries, key_heads, preferred_element_type=jnp.float32)
        * score_scale
    )
    row_top = jnp.max(raw, axis=-1)
    log_total = row_top + jnp.log(jnp.sum(jnp.exp(raw - row_top[..., None]), axis=-1))
    attn_probs = jnp.exp(raw - log_total[..., None]).astype(jnp.bfloat16)
    heads_out = jnp.einsum(
        "bhqk,bkhe->bqhe", attn_probs, value_heads, preferred_element_type=jnp.float32
    )
    heads_out = heads_out.astype(jnp.bfloat16).reshape(tokens, local_width)
    merge_terms = jnp.dot(heads_out, attn_merge, preferred_element_type=jnp.float32)
    middle = wide_input + lax.psum(merge_terms.astype(jnp.bfloat16), "tensor").astype(jnp.float32)
    normed_two, inverse_two = norm_parts(middle)
    second_in = (normed_two * mixer_gain).astype(jnp.bfloat16)
    logits = jnp.dot(second_in, router_weight, preferred_element_type=jnp.float32)
    labels = jnp.arange(experts, dtype=jnp.int32)
    first_hot = (routes[:, 0:1] == labels[None, :]).astype(jnp.float32)
    second_hot = (routes[:, 1:2] == labels[None, :]).astype(jnp.float32)
    gate_first = jax.nn.sigmoid(jnp.sum(logits * (first_hot - second_hot), axis=1))
    kept = keep_mask.astype(jnp.float32)
    gate_weights = jnp.stack([gate_first, 1.0 - gate_first], axis=1) * kept
    slots = slot_table(routes, keep_mask, experts)
    live_mask = keep_mask > 0
    target = jnp.where(live_mask, routes * capacity + slots, experts * capacity).reshape(-1)
    source = jnp.where(live_mask, routes * capacity + slots, 0)
    send_rows = (
        jnp.zeros((experts * capacity, D), jnp.bfloat16)
        .at[target]
        .set(jnp.repeat(second_in, 2, axis=0), mode="drop")
    )
    arrived = spread_rows(send_rows, experts, capacity)
    pre_act = jnp.dot(arrived, expert_up[0], preferred_element_type=jnp.float32)
    hidden = gelu_value(pre_act).astype(jnp.bfloat16)
    partial_terms = jnp.dot(hidden, expert_down[0], preferred_element_type=jnp.float32)
    expert_rows = return_rows(partial_terms, experts, capacity)
    picked = expert_rows[source] * kept[:, :, None]
    mixed_rows = jnp.sum(gate_weights[:, :, None] * picked, axis=1)
    moe = lax.psum(mixed_rows.astype(jnp.bfloat16), "tensor").astype(jnp.float32)
    block_output = (middle + moe).astype(jnp.bfloat16)
    grad_wide = out_grad.astype(jnp.float32)
    d_rows = (
        (gate_weights[:, :, None] * grad_wide[:, None, :])
        .astype(jnp.bfloat16)
        .reshape(tokens * 2, D)
    )
    d_send = jnp.zeros((experts * capacity, D), jnp.bfloat16).at[target].set(d_rows, mode="drop")
    d_arrived = spread_rows(d_send, experts, capacity)
    d_hidden = lax.dot_general(
        d_arrived, expert_down[0], (((1,), (1,)), ((), ())), preferred_element_type=jnp.float32
    )
    down_local = lax.dot_general(
        hidden, d_arrived, (((0,), (0,)), ((), ())), preferred_element_type=jnp.float32
    )
    d_pre = (d_hidden * gelu_slope(pre_act)).astype(jnp.bfloat16)
    up_local = lax.dot_general(
        arrived, d_pre, (((0,), (0,)), ((), ())), preferred_element_type=jnp.float32
    )
    d_terms = lax.dot_general(
        d_pre, expert_up[0], (((1,), (1,)), ((), ())), preferred_element_type=jnp.float32
    )
    d_back = return_rows(d_terms, experts, capacity)
    d_picked = jnp.sum(d_back[source] * kept[:, :, None], axis=1)
    dots_part = jnp.sum(picked * grad_wide[:, None, :], axis=2)
    d_moe, gate_dots = (
        lax.psum(d_picked.astype(jnp.bfloat16), "tensor").astype(jnp.float32),
        lax.psum(dots_part.astype(jnp.bfloat16), "tensor").astype(jnp.float32),
    )
    d_gates = gate_dots * kept
    d_diff = (d_gates[:, 0] - d_gates[:, 1]) * gate_first * (1.0 - gate_first)
    d_logits = (d_diff[:, None] * (first_hot - second_hot)).astype(jnp.bfloat16)
    router_part = lax.dot_general(
        second_in, d_logits, (((0,), (0,)), ((), ())), preferred_element_type=jnp.float32
    )
    d_second = d_moe + lax.dot_general(
        d_logits, router_weight, (((1,), (1,)), ((), ())), preferred_element_type=jnp.float32
    )
    mixer_part = jnp.sum(d_second * normed_two, axis=0)
    d_middle = grad_wide + norm_back(d_second, normed_two, inverse_two, mixer_gain)
    d_low = d_middle.astype(jnp.bfloat16)
    merge_local = lax.dot_general(
        heads_out, d_low, (((0,), (0,)), ((), ())), preferred_element_type=jnp.float32
    )
    d_heads = lax.dot_general(
        d_low, attn_merge, (((1,), (1,)), ((), ())), preferred_element_type=jnp.float32
    ).astype(jnp.bfloat16)
    d_grid = d_heads.reshape(IMG_DEV, SEQ, heads_here, HEAD)
    out_grid = heads_out.reshape(IMG_DEV, SEQ, heads_here, HEAD)
    delta = jnp.einsum("bqhe,bqhe->bhq", d_grid, out_grid, preferred_element_type=jnp.float32)
    raw_again = (
        jnp.einsum("bqhe,bkhe->bhqk", queries, key_heads, preferred_element_type=jnp.float32)
        * score_scale
    )
    probs_wide = jnp.exp(raw_again - log_total[..., None])
    probs_low = probs_wide.astype(jnp.bfloat16)
    d_probs = jnp.einsum("bqhe,bkhe->bhqk", d_grid, value_heads, preferred_element_type=jnp.float32)
    d_raw = (probs_wide * (d_probs - delta[..., None]) * score_scale).astype(jnp.bfloat16)
    d_queries = jnp.einsum("bhqk,bkhe->bqhe", d_raw, key_heads, preferred_element_type=jnp.float32)
    d_keys = jnp.einsum("bhqk,bqhe->bkhe", d_raw, queries, preferred_element_type=jnp.float32)
    d_values = jnp.einsum("bhqk,bqhe->bkhe", probs_low, d_grid, preferred_element_type=jnp.float32)
    d_proj = (
        jnp.stack([d_queries, d_keys, d_values], axis=2)
        .astype(jnp.bfloat16)
        .reshape(tokens, 3, local_width)
    )
    proj_local = jnp.einsum("td,tce->dce", first_in, d_proj, preferred_element_type=jnp.float32)
    first_terms = jnp.einsum("tce,dce->td", d_proj, attn_proj, preferred_element_type=jnp.float32)
    d_first = lax.psum(first_terms.astype(jnp.bfloat16), "tensor").astype(jnp.float32)
    input_grad = d_middle + norm_back(d_first, normed_one, inverse_one, attn_gain)
    attn_part = jnp.sum(d_first * normed_one, axis=0)
    proj_grad, merge_grad, router_grad, attn_gain_grad, mixer_gain_grad = lax.psum(
        (proj_local, merge_local, router_part, attn_part, mixer_part), "expert"
    )
    return (
        block_output,
        input_grad,
        attn_gain_grad,
        proj_grad,
        merge_grad,
        mixer_gain_grad,
        router_grad,
        up_local[None],
        down_local[None],
    )

MESH = pl.DeviceIdType.MESH
VMEM_LIMIT = 60 * 1024 * 1024


class Net:
    def __init__(self, sizes):
        e = lax.axis_index("expert")
        t = lax.axis_index("tensor")
        self.sizes = sizes
        self.at = [e // sizes[1], e % sizes[1], t // sizes[3], t % sizes[3]]

    def shift(self, rel):
        return [(a + r) % s if r else a for a, r, s in zip(self.at, rel, self.sizes)]

    def ident(self, place):
        return (place[0] * self.sizes[1] + place[1], place[2] * self.sizes[3] + place[3])

    def peers(self, dims):
        found = []
        for d in dims:
            for j in range(1, self.sizes[d]):
                rel = [0, 0, 0, 0]
                rel[d] = j
                found.append(self.ident(self.shift(rel)))
        return found

    def enter(self, dims):
        barrier = pltpu.get_barrier_semaphore()
        near = self.peers(dims)
        for peer in near:
            pl.semaphore_signal(barrier, inc=1, device_id=peer, device_id_type=MESH)
        pl.semaphore_wait(barrier, len(near))


def slot_of(rel, sizes, dims):
    index = 0
    for d in dims:
        index = index * sizes[d] + rel[d] % sizes[d]
    return index


def spread(net, own, out, send, recv, order):
    sizes = net.sizes
    dims = sorted(order)
    sent = []

    def block(rel):
        place = net.shift(rel)
        index = 0
        for d in dims:
            index = index * sizes[d] + place[d]
        return index

    def copy_of(source, rel, d, j):
        there = list(rel)
        there[d] = there[d] - j
        step = [0, 0, 0, 0]
        step[d] = j
        return pltpu.make_async_remote_copy(
            src_ref=source,
            dst_ref=out.at[block(rel)],
            send_sem=send.at[len(sent)],
            recv_sem=recv.at[slot_of(there, sizes, dims)],
            device_id=net.ident(net.shift(step)),
            device_id_type=MESH,
        )

    def forward(source, rel, later):
        for d in later:
            for j in range(1, sizes[d]):
                copy = copy_of(source, rel, d, j)
                copy.start()
                sent.append(copy)

    zero = (0, 0, 0, 0)
    forward(own, zero, order)
    out[block(zero)] = own[...]
    yield
    held = [zero]
    for k, d in enumerate(order):
        fresh = []
        for base in held:
            for j in range(1, sizes[d]):
                rel = list(base)
                rel[d] = j
                here = out.at[block(rel)]
                pltpu.make_async_remote_copy(
                    src_ref=here,
                    dst_ref=here,
                    send_sem=send.at[0],
                    recv_sem=recv.at[slot_of(rel, sizes, dims)],
                    device_id=net.peers([d])[0],
                    device_id_type=MESH,
                ).wait_recv()
                forward(here, rel, order[k + 1 :])
                fresh.append(tuple(rel))
        held = held + fresh
        yield
    for copy in sent:
        copy.wait_send()


def together(steps):
    live = list(steps)
    while live:
        left = []
        for step in live:
            try:
                next(step)
                left.append(step)
            except StopIteration:
                pass
        live = left


def count_of(sizes, order):
    total = 1
    for d in order:
        total *= sizes[d]
    return total


def params(cid):
    return pltpu.CompilerParams(
        collective_id=cid, has_side_effects=True, vmem_limit_bytes=VMEM_LIMIT
    )


def vmem(count):
    return [pl.BlockSpec(memory_space=pltpu.VMEM)] * count


def gather_kernel(sizes, orders, *refs):
    n = len(orders)
    net = Net(sizes)
    net.enter(sorted({d for order in orders for d in order}))
    ins, outs, sems = refs[:n], refs[n : 2 * n], refs[2 * n :]
    together(
        [
            spread(net, ins[i], outs[i], sems[2 * i], sems[2 * i + 1], orders[i])
            for i in range(n)
        ]
    )


def gather_call(sizes, cid, arrays, orders):
    counts = [count_of(sizes, order) for order in orders]
    sems = []
    for count in counts:
        sems += [pltpu.SemaphoreType.DMA((count - 1,)), pltpu.SemaphoreType.DMA((count,))]
    return pl.pallas_call(
        functools.partial(gather_kernel, sizes, orders),
        out_shape=[
            jax.ShapeDtypeStruct((count,) + a.shape, a.dtype) for count, a in zip(counts, arrays)
        ],
        in_specs=vmem(len(arrays)),
        out_specs=vmem(len(arrays)),
        scratch_shapes=sems,
        compiler_params=params(cid),
    )(*arrays)


def scatter_tensor(net, terms, landed, send, recv):
    sizes = net.sizes
    sent = []
    index = 0
    for jx in range(sizes[2]):
        for jc in range(sizes[3]):
            if jx == 0 and jc == 0:
                continue
            place = net.shift((0, 0, jx, jc))
            back = slot_of((0, 0, -jx, -jc), sizes, (2, 3)) - 1
            copy = pltpu.make_async_remote_copy(
                src_ref=terms.at[place[2] * sizes[3] + place[3]],
                dst_ref=landed.at[back],
                send_sem=send.at[index],
                recv_sem=recv.at[back],
                device_id=net.ident(place),
                device_id_type=MESH,
            )
            copy.start()
            sent.append((copy, back))
            index += 1
    return sent


def scatter_finish(net, terms, landed, sent):
    own = net.at[2] * net.sizes[3] + net.at[3]
    total = terms[own].astype(jnp.float32)
    for copy, slot in sent:
        copy.wait()
    for slot in range(len(sent)):
        total = total + landed[slot].astype(jnp.float32)
    return total


def tensor_peers_enter(net, extra, experts=False):
    barrier = pltpu.get_barrier_semaphore()
    near = []
    for jx in range(net.sizes[2]):
        for jc in range(net.sizes[3]):
            if jx or jc:
                near.append(net.ident(net.shift((0, 0, jx, jc))))
    near = near + net.peers(extra)
    if experts:
        for jz in range(net.sizes[0]):
            for jy in range(net.sizes[1]):
                if jz or jy:
                    near.append(net.ident(net.shift((jz, jy, 0, 0))))
    for peer in near:
        pl.semaphore_signal(barrier, inc=1, device_id=peer, device_id_type=MESH)
    pl.semaphore_wait(barrier, len(near))


def merge_kernel(sizes, terms, out, landed, send, recv):
    net = Net(sizes)
    tensor_peers_enter(net, ())
    sent = scatter_tensor(net, terms, landed, send, recv)
    out[...] = scatter_finish(net, terms, landed, sent)


def merge_call(sizes, cid, terms):
    tensor = terms.shape[0]
    return pl.pallas_call(
        functools.partial(merge_kernel, sizes),
        out_shape=jax.ShapeDtypeStruct(terms.shape[1:], jnp.float32),
        in_specs=vmem(1),
        out_specs=pl.BlockSpec(memory_space=pltpu.VMEM),
        scratch_shapes=[
            pltpu.VMEM((tensor - 1,) + terms.shape[1:], terms.dtype),
            pltpu.SemaphoreType.DMA((tensor - 1,)),
            pltpu.SemaphoreType.DMA((tensor - 1,)),
        ],
        compiler_params=params(cid),
    )(terms)


def fold(net, part, out, core_in, core_sum, mid_in, mid_sum, low_in, low_sum, z_in, sems, x_first):
    z, y, x, c = net.at
    depth = net.sizes[0]
    kind = part.dtype
    wide = jnp.float32
    core_peer = net.peers([3])[0]
    first_dim, second_dim = (2, 1) if x_first else (1, 2)
    mid_peer, low_peer = net.peers([first_dim])[0], net.peers([second_dim])[0]
    first_at, second_at = net.at[first_dim], net.at[second_dim]

    def remote(source, target, stage, index, landing, peer):
        return pltpu.make_async_remote_copy(
            src_ref=source,
            dst_ref=target,
            send_sem=sems.at[stage, 0, index],
            recv_sem=sems.at[stage, 1, landing],
            device_id=peer,
            device_id_type=MESH,
        )

    zs = [(z + 1 + k) % depth if k < depth - 1 else z for k in range(depth)]
    core, mid, low, far = [], [], [], []
    for k in range(depth):
        copy = remote(part.at[zs[k], :, :, 1 - c], core_in.at[k], 0, k, k, core_peer)
        copy.start()
        core.append(copy)
    yield
    for k in range(depth):
        core[k].wait_recv()
        core_sum[k] = (part[zs[k], :, :, c].astype(wide) + core_in[k].astype(wide)).astype(kind)
        away = core_sum.at[k, :, 1 - first_at] if x_first else core_sum.at[k, 1 - first_at]
        copy = remote(away, mid_in.at[k], 1, k, k, mid_peer)
        copy.start()
        mid.append(copy)
    yield
    for k in range(depth):
        mid[k].wait_recv()
        near = core_sum[k, :, first_at] if x_first else core_sum[k, first_at]
        mid_sum[k] = (near.astype(wide) + mid_in[k].astype(wide)).astype(kind)
        copy = remote(mid_sum.at[k, 1 - second_at], low_in.at[k], 2, k, k, low_peer)
        copy.start()
        low.append(copy)
    yield
    for k in range(depth):
        low[k].wait_recv()
        total = mid_sum[k, second_at].astype(wide) + low_in[k].astype(wide)
        if k == depth - 1:
            out[...] = total
        else:
            low_sum[k] = total.astype(kind)
            landing = depth - k - 2
            peer = net.ident([zs[k], y, x, c])
            copy = remote(low_sum.at[k], z_in.at[landing], 3, k, landing, peer)
            copy.start()
            far.append(copy)
    yield
    for k in range(depth - 1):
        far[k].wait_recv()
    total = out[...]
    for k in range(depth - 1):
        total = total + z_in[k].astype(wide)
    out[...] = total
    for copy in core + mid + low + far:
        copy.wait_send()


def fold_scratch(sizes, shape, kind):
    depth, ys, xs, cs = sizes
    return [
        pltpu.VMEM((depth, ys, xs) + shape, kind),
        pltpu.VMEM((depth, ys, xs) + shape, kind),
        pltpu.VMEM((depth, 2) + shape, kind),
        pltpu.VMEM((depth, 2) + shape, kind),
        pltpu.VMEM((depth,) + shape, kind),
        pltpu.VMEM((depth - 1,) + shape, kind),
        pltpu.VMEM((depth - 1,) + shape, kind),
        pltpu.SemaphoreType.DMA((4, 2, depth)),
    ]


def fold_kernel(sizes, firsts, *refs):
    n = len(firsts)
    net = Net(sizes)
    net.enter((0, 1, 2, 3))
    ins, outs, rest = refs[:n], refs[n : 2 * n], refs[2 * n :]
    together(
        [
            fold(net, ins[i], outs[i], *rest[8 * i : 8 * i + 8], firsts[i])
            for i in range(n)
        ]
    )


def fold_call(sizes, cid, arrays, firsts):
    shaped = [a.reshape(tuple(sizes) + a.shape[1:]) for a in arrays]
    scratch = []
    for a in arrays:
        scratch += fold_scratch(sizes, a.shape[1:], a.dtype)
    return pl.pallas_call(
        functools.partial(fold_kernel, sizes, firsts),
        out_shape=[jax.ShapeDtypeStruct(a.shape[1:], jnp.float32) for a in arrays],
        in_specs=vmem(len(arrays)),
        out_specs=vmem(len(arrays)),
        scratch_shapes=scratch,
        compiler_params=params(cid),
    )(*shaped)


def ring(net, part, y_in, y_sum, z_in, total, own, out, sems, send, recv):
    z, y, x, c = net.at
    depth = net.sizes[0]
    kind = part.dtype
    wide = jnp.float32
    y_peer = net.peers([1])[0]
    zs = [(z + 1 + k) % depth if k < depth - 1 else z for k in range(depth)]
    near, far = [], []

    def remote(source, target, stage, index, landing, peer):
        return pltpu.make_async_remote_copy(
            src_ref=source,
            dst_ref=target,
            send_sem=sems.at[stage, 0, index],
            recv_sem=sems.at[stage, 1, landing],
            device_id=peer,
            device_id_type=MESH,
        )

    for k in range(depth):
        copy = remote(part.at[zs[k], 1 - y], y_in.at[k], 0, k, k, y_peer)
        copy.start()
        near.append(copy)
    yield
    for k in range(depth):
        near[k].wait_recv()
        here = part[zs[k], y].astype(wide) + y_in[k].astype(wide)
        if k == depth - 1:
            total[...] = here
        else:
            y_sum[k] = here.astype(kind)
            landing = depth - k - 2
            peer = net.ident([zs[k], y, x, c])
            copy = remote(y_sum.at[k], z_in.at[landing], 1, k, landing, peer)
            copy.start()
            far.append(copy)
    yield
    for k in range(depth - 1):
        far[k].wait_recv()
    done = total[...]
    for k in range(depth - 1):
        done = done + z_in[k].astype(wide)
    own[...] = done.astype(kind)
    yield
    yield from spread(net, own, out, send, recv, (0, 1))
    for copy in near + far:
        copy.wait_send()


def ring_scratch(sizes, shape, kind):
    depth = sizes[0]
    count = depth * sizes[1]
    return [
        pltpu.VMEM((depth,) + shape, kind),
        pltpu.VMEM((depth - 1,) + shape, kind),
        pltpu.VMEM((depth - 1,) + shape, kind),
        pltpu.VMEM(shape, jnp.float32),
        pltpu.VMEM(shape, kind),
        pltpu.SemaphoreType.DMA((2, 2, depth)),
        pltpu.SemaphoreType.DMA((count - 1,)),
        pltpu.SemaphoreType.DMA((count,)),
    ]


def tail_kernel(sizes, gain_row, *refs):
    terms, d_middle, normed, inverse, gain, small, proj, merge = refs[:8]
    grad_all, proj_all, merge_all, small_out = refs[8:12]
    rest = refs[12:]
    landed, grad_own, small_in, small_sum, sc_send, sc_recv, g_send, g_recv, s_send, s_recv = rest[
        :10
    ]
    ring_one, ring_two = rest[10:18], rest[18:26]
    net = Net(sizes)
    tensor_peers_enter(net, (), True)
    sent = scatter_tensor(net, terms, landed, sc_send, sc_recv)
    rings = [
        ring(net, proj, *ring_one[:5], proj_all, *ring_one[5:]),
        ring(net, merge, *ring_two[:5], merge_all, *ring_two[5:]),
    ]
    for step in rings:
        next(step)
    for step in rings:
        next(step)
    d_first = scatter_finish(net, terms, landed, sent)
    scaled = d_first * gain[...]
    plain = normed[...]
    mean = jnp.mean(scaled, axis=-1, keepdims=True)
    mixed = jnp.mean(scaled * plain, axis=-1, keepdims=True)
    grad = d_middle[...] + inverse[...] * (scaled - mean - plain * mixed)
    grad_own[...] = grad.astype(jnp.bfloat16)
    part = jnp.sum(d_first * plain, axis=0, keepdims=True)
    row = lax.broadcasted_iota(jnp.int32, small.shape, 0)
    small_sum[0] = jnp.where(row == gain_row, part, small[...])
    copies = []

    def exchange(stage, slot, landing, place):
        copy = pltpu.make_async_remote_copy(
            src_ref=small_sum.at[stage],
            dst_ref=small_in.at[landing],
            send_sem=s_send.at[slot],
            recv_sem=s_recv.at[landing],
            device_id=net.ident(place),
            device_id_type=MESH,
        )
        copy.start()
        copies.append(copy)
        return copy

    exchange(0, 0, 0, net.shift((0, 0, 0, 1))).wait_recv()
    small_sum[1] = small_sum[0] + small_in[0]
    exchange(1, 1, 1, net.shift((0, 0, 1, 0))).wait_recv()
    small_sum[2] = small_sum[1] + small_in[1]
    grad_step = spread(net, grad_own, grad_all, g_send, g_recv, (2, 3))
    next(grad_step)
    slot = 2
    final = []
    for jz in range(sizes[0]):
        for jy in range(sizes[1]):
            if jz or jy:
                landing = 1 + slot_of((-jz, -jy, 0, 0), sizes, (0, 1))
                final.append(exchange(2, slot, landing, net.shift((jz, jy, 0, 0))))
                slot += 1
    for step in rings:
        next(step)
    for step in rings:
        next(step)
    next(grad_step)
    for step in rings:
        next(step)
    for copy in final:
        copy.wait_recv()
    total = small_sum[2]
    for k in range(len(final)):
        total = total + small_in[2 + k]
    small_out[...] = total
    for copy in copies:
        copy.wait_send()
    together([grad_step] + rings)


def tail_call(sizes, cid, gain_row, terms, d_middle, normed, inverse, gain, small, proj, merge):
    experts_axis, tensor = sizes[0] * sizes[1], sizes[2] * sizes[3]
    steps = 1 + experts_axis
    dma = pltpu.SemaphoreType.DMA
    shape = d_middle.shape
    low = jnp.bfloat16
    split = tuple(sizes[:2])
    proj = proj.reshape(split + (proj.shape[0] // experts_axis,) + proj.shape[1:])
    merge = merge.reshape(split + (merge.shape[0] // experts_axis,) + merge.shape[1:])
    return pl.pallas_call(
        functools.partial(tail_kernel, sizes, gain_row),
        out_shape=[
            jax.ShapeDtypeStruct((tensor,) + shape, low),
            jax.ShapeDtypeStruct((experts_axis,) + proj.shape[2:], low),
            jax.ShapeDtypeStruct((experts_axis,) + merge.shape[2:], low),
            jax.ShapeDtypeStruct(small.shape, jnp.float32),
        ],
        in_specs=vmem(8),
        out_specs=vmem(4),
        scratch_shapes=[
            pltpu.VMEM((tensor - 1,) + shape, low),
            pltpu.VMEM(shape, low),
            pltpu.VMEM((steps,) + small.shape, jnp.float32),
            pltpu.VMEM((3,) + small.shape, jnp.float32),
            dma((tensor - 1,)),
            dma((tensor - 1,)),
            dma((tensor - 1,)),
            dma((tensor,)),
            dma((steps,)),
            dma((steps,)),
        ]
        + ring_scratch(sizes, proj.shape[2:], low)
        + ring_scratch(sizes, merge.shape[2:], low),
        compiler_params=params(cid),
    )(terms, d_middle, normed, inverse, gain, small, proj, merge)


def on_device_dense(
    sizes,
    block_input,
    attn_gain,
    attn_proj,
    attn_merge,
    mixer_gain,
    router_weight,
    expert_up,
    expert_down,
    routes,
    keep_mask,
    out_grad,
):
    experts_axis, tensor = sizes[0] * sizes[1], sizes[2] * sizes[3]
    experts = experts_axis // PAIR
    tokens = block_input.shape[0]
    rows = -(-(-(-tokens // tensor)) // 8) * 8
    padded = rows * tensor
    local_width = attn_proj.shape[2]
    heads_here = local_width // HEAD
    score_scale = HEAD ** (-0.5)
    start = lax.axis_index("tensor") * rows
    low = jnp.bfloat16
    wide = jnp.float32

    def fill(array):
        return jnp.pad(array, ((0, padded - tokens), (0, 0)))

    def quarter(array):
        return lax.dynamic_slice_in_dim(array, start, rows, axis=0)

    input_q = quarter(fill(block_input)).astype(wide)
    grad_q_low = quarter(fill(out_grad))
    grad_q = grad_q_low.astype(wide)
    route_q = quarter(fill(routes))
    keep_q = quarter(fill(keep_mask))

    normed_one, unused = norm_parts(block_input.astype(wide))
    first_in = (normed_one * attn_gain).astype(low)
    normed_q, inverse_q = norm_parts(input_q)
    proj = jnp.einsum("td,dce->tce", first_in, attn_proj, preferred_element_type=wide).astype(low)
    head_grid = proj.reshape(tokens, 3, heads_here, HEAD)
    queries, key_heads, value_heads = head_grid[:, 0], head_grid[:, 1], head_grid[:, 2]
    raw = jnp.einsum("qhe,khe->hqk", queries, key_heads, preferred_element_type=wide) * score_scale
    row_top = jnp.max(raw, axis=-1, keepdims=True)
    powers = jnp.exp(raw - row_top)
    probs_wide = powers / jnp.sum(powers, axis=-1, keepdims=True)
    probs_low = probs_wide.astype(low)
    heads_out = jnp.einsum("hqk,khe->qhe", probs_low, value_heads, preferred_element_type=wide)
    heads_out = heads_out.astype(low).reshape(tokens, local_width)
    merge_terms = jnp.dot(fill(heads_out), attn_merge, preferred_element_type=wide).astype(low)

    merged = merge_call(sizes, 1, merge_terms.reshape(tensor, rows, D))
    middle = input_q + merged
    normed_two, inverse_two = norm_parts(middle)
    second_q = (normed_two * mixer_gain).astype(low)

    codes = jnp.concatenate([route_q, keep_q], axis=1).astype(wide).T
    codes = jnp.pad(codes, ((0, 4), (0, -rows % 128)))
    everywhere = (0, 1, 2, 3)
    second_all, grad_all, codes_all = gather_call(
        sizes,
        2,
        [second_q, grad_q_low, codes],
        [everywhere, (0, 2, 1, 3), everywhere],
    )
    total = experts_axis * padded
    arrived = second_all.reshape(total, D)
    grads = grad_all.reshape(total, D)

    label = lax.axis_index("expert") // PAIR
    code = codes_all[:, :4, :rows].transpose(0, 2, 1).reshape(total, 4)
    labels = jnp.arange(experts, dtype=wide)
    pick_all = (code[:, 0:1] == labels).astype(wide) - (code[:, 1:2] == labels).astype(wide)
    logits_all = jnp.dot(arrived, router_weight, preferred_element_type=wide)
    gate_all = jax.nn.sigmoid(jnp.sum(logits_all * pick_all, axis=1, keepdims=True))
    live_first = jnp.where(code[:, 0:1] == label.astype(wide), code[:, 2:3], 0.0)
    live_second = jnp.where(code[:, 1:2] == label.astype(wide), code[:, 3:4], 0.0)
    weight = live_first * gate_all + live_second * (1.0 - gate_all)
    side = live_first - live_second

    up, down = expert_up[0], expert_down[0]
    pre_act = jnp.dot(arrived, up, preferred_element_type=wide)
    hidden = gelu_value(pre_act).astype(low)
    partial_terms = jnp.dot(hidden, down, preferred_element_type=wide)
    moe_terms = (weight * partial_terms).astype(low)
    dots = jnp.sum(
        (partial_terms * grads.astype(wide)).reshape(experts_axis * tensor, rows, D), axis=2
    ) * side.reshape(experts_axis * tensor, rows)
    dots = jnp.broadcast_to(
        jnp.pad(dots, ((0, 0), (0, -rows % 128)))[:, None, :],
        (experts_axis * tensor, 8, -(-rows // 128) * 128),
    )
    d_rows = (weight * grads.astype(wide)).astype(low)
    d_hidden = lax.dot_general(d_rows, down, (((1,), (1,)), ((), ())), preferred_element_type=wide)
    down_local = lax.dot_general(
        hidden, d_rows, (((0,), (0,)), ((), ())), preferred_element_type=wide
    )
    d_pre = (d_hidden * gelu_slope(pre_act)).astype(low)
    up_local = lax.dot_general(arrived, d_pre, (((0,), (0,)), ((), ())), preferred_element_type=wide)
    d_terms = lax.dot_general(
        d_pre, up, (((1,), (1,)), ((), ())), preferred_element_type=wide
    ).astype(low)

    shape = (experts_axis * tensor, rows, D)
    moe, d_moe, dots_sum = fold_call(
        sizes,
        3,
        [moe_terms.reshape(shape), d_terms.reshape(shape), dots],
        (True, False, True),
    )
    block_q = (middle + moe).astype(low)
    mine = jnp.arange(experts, dtype=jnp.int32)
    pick = (route_q[:, 0:1] == mine).astype(wide) - (route_q[:, 1:2] == mine).astype(wide)
    logits = jnp.dot(second_q, router_weight, preferred_element_type=wide)
    gate_first = jax.nn.sigmoid(jnp.sum(logits * pick, axis=1))
    d_diff = dots_sum[0, :rows] * gate_first * (1.0 - gate_first)
    d_logits = (d_diff[:, None] * pick).astype(low)
    router_part = lax.dot_general(
        d_logits, second_q, (((0,), (0,)), ((), ())), preferred_element_type=wide
    )
    d_second = d_moe + lax.dot_general(
        d_logits, router_weight, (((1,), (1,)), ((), ())), preferred_element_type=wide
    )
    mixer_part = jnp.sum(d_second * normed_two, axis=0, keepdims=True)
    d_middle = grad_q + norm_back(d_second, normed_two, inverse_two, mixer_gain)
    d_low_q = d_middle.astype(low)

    low_rows, block_rows = gather_call(sizes, 4, [d_low_q, block_q], [(2, 3), (2, 3)])
    d_low = low_rows.reshape(padded, D)[:tokens]
    block_output = block_rows.reshape(padded, D)[:tokens]

    d_heads = lax.dot_general(
        d_low, attn_merge, (((1,), (1,)), ((), ())), preferred_element_type=wide
    ).astype(low)
    d_grid = d_heads.reshape(tokens, heads_here, HEAD)
    out_grid = heads_out.reshape(tokens, heads_here, HEAD)
    delta = jnp.sum(d_grid.astype(wide) * out_grid.astype(wide), axis=2).T
    d_probs = jnp.einsum("qhe,khe->hqk", d_grid, value_heads, preferred_element_type=wide)
    d_raw = (probs_wide * (d_probs - delta[..., None]) * score_scale).astype(low)
    d_queries = jnp.einsum("hqk,khe->qhe", d_raw, key_heads, preferred_element_type=wide)
    d_keys = jnp.einsum("hqk,qhe->khe", d_raw, queries, preferred_element_type=wide)
    d_values = jnp.einsum("hqk,qhe->khe", probs_low, d_grid, preferred_element_type=wide)
    d_proj = jnp.concatenate(
        [part.astype(low).reshape(tokens, local_width) for part in (d_queries, d_keys, d_values)],
        axis=1,
    )
    flat_proj = attn_proj.reshape(D, 3 * local_width)
    first_terms = lax.dot_general(
        fill(d_proj), flat_proj, (((1,), (1,)), ((), ())), preferred_element_type=wide
    ).astype(low)
    small = jnp.concatenate([router_part, mixer_part], axis=0)
    small = jnp.pad(small, ((0, 1 + -(experts + 2) % 8), (0, 0)))
    proj_local = lax.dot_general(
        first_in, d_proj, (((0,), (0,)), ((), ())), preferred_element_type=wide
    ).astype(low)
    merge_local = lax.dot_general(
        heads_out, d_low, (((0,), (0,)), ((), ())), preferred_element_type=wide
    ).astype(low)
    grad_rows, proj_all, merge_all, small_all = tail_call(
        sizes,
        5,
        experts + 1,
        first_terms.reshape(tensor, rows, D),
        d_middle,
        normed_q,
        inverse_q,
        attn_gain[None, :],
        small,
        proj_local,
        merge_local,
    )
    input_grad = grad_rows.reshape(padded, D)[:tokens].astype(wide)
    proj_grad = proj_all.astype(wide).reshape(D, 3, local_width)
    merge_grad = merge_all.astype(wide).reshape(local_width, D)
    return (
        block_output,
        input_grad,
        small_all[experts + 1],
        proj_grad,
        merge_grad,
        small_all[experts],
        small_all[:experts].T,
        up_local[None],
        down_local[None],
    )


def program_of(mesh):
    experts_axis, tensor = mesh.shape["expert"], mesh.shape["tensor"]
    if tensor != 4 or experts_axis % 2 or experts_axis < 4:
        return on_device
    capacity = max(8, 4 * TOK_DEV // (experts_axis // PAIR) // 8 * 8)
    rows = -(-(-(-TOK_DEV // tensor)) // 8) * 8
    if 4 * rows * tensor > 5 * capacity:
        return on_device
    return functools.partial(on_device_dense, (experts_axis // 2, 2, tensor // 2, 2))


def solution(mesh):
    in_specs = (
        P("expert", None),
        P(),
        P(None, None, "tensor"),
        P("tensor", None),
        P(),
        P(),
        P("expert", None, "tensor"),
        P("expert", "tensor", None),
        P("expert", None),
        P("expert", None),
        P("expert", None),
    )
    out_specs = (
        P("expert", None),
        P("expert", None),
        P(),
        P(None, None, "tensor"),
        P("tensor", None),
        P(),
        P(),
        P("expert", None, "tensor"),
        P("expert", "tensor", None),
    )
    return jax.shard_map(
        program_of(mesh), mesh=mesh, in_specs=in_specs, out_specs=out_specs, check_vma=False
    )
```

```python
import functools

import jax
import jax.numpy as jnp
from jax import lax
from jax.experimental import pallas as pl
from jax.experimental.pallas import tpu as pltpu
from jax.sharding import PartitionSpec as P

D = 768
SEQ = 197
PAIR = 2
IMG_DEV = 1
HEAD = 64
TOK_DEV = 197


EPS = 1e-06
ROOT_HALF = 0.7071067811865476
INV_ROOT_TAU = 0.3989422804014327


def norm_parts(values):
    center = values - jnp.mean(values, axis=-1, keepdims=True)
    inverse = lax.rsqrt(jnp.mean(center * center, axis=-1, keepdims=True) + EPS)
    return (center * inverse, inverse)


def norm_back(upstream, normed, inverse, gain):
    scaled = upstream * gain
    return inverse * (
        scaled
        - jnp.mean(scaled, axis=-1, keepdims=True)
        - normed * jnp.mean(scaled * normed, axis=-1, keepdims=True)
    )


def gelu_value(pre_act):
    return 0.5 * pre_act * (1.0 + lax.erf(pre_act * ROOT_HALF))


def gelu_slope(pre_act):
    return (
        0.5 * (1.0 + lax.erf(pre_act * ROOT_HALF))
        + pre_act * jnp.exp(-0.5 * pre_act * pre_act) * INV_ROOT_TAU
    )


def slot_table(routes, keep_mask, experts):
    labels = jnp.arange(experts, dtype=jnp.int32)
    chosen = routes[:, :, None] == labels[None, None, :]
    hits = jnp.where(chosen & (keep_mask[:, :, None] > 0), 1, 0).astype(jnp.int32)
    per_token = jnp.sum(hits, axis=1)
    before = jnp.cumsum(per_token, axis=0) - per_token
    return jnp.sum(jnp.where(chosen, before[:, None, :], 0), axis=2)


def spread_rows(slot_rows, experts, capacity):
    width = slot_rows.shape[-1]
    paired = jnp.broadcast_to(
        slot_rows.reshape(experts, 1, capacity, width), (experts, PAIR, capacity, width)
    )
    paired = paired.reshape(experts * PAIR, capacity, width)
    arrived = lax.all_to_all(paired, "expert", split_axis=0, concat_axis=0, tiled=True)
    return arrived.reshape(-1, width)


def return_rows(partial_terms, experts, capacity):
    width = partial_terms.shape[-1]
    sent_rows = partial_terms.astype(jnp.bfloat16).reshape(experts * PAIR, capacity, width)
    landed = lax.all_to_all(sent_rows, "expert", split_axis=0, concat_axis=0, tiled=True).astype(
        jnp.float32
    )
    return jnp.sum(landed.reshape(experts, PAIR, capacity, width), axis=1).reshape(
        experts * capacity, width
    )


def on_device(
    block_input,
    attn_gain,
    attn_proj,
    attn_merge,
    mixer_gain,
    router_weight,
    expert_up,
    expert_down,
    routes,
    keep_mask,
    out_grad,
):
    experts = lax.axis_size("expert") // PAIR
    capacity = max(8, 4 * TOK_DEV // experts // 8 * 8)
    local_width = attn_proj.shape[2]
    heads_here = local_width // HEAD
    score_scale = HEAD ** (-0.5)
    tokens = block_input.shape[0]
    wide_input = block_input.astype(jnp.float32)
    normed_one, inverse_one = norm_parts(wide_input)
    first_in = (normed_one * attn_gain).astype(jnp.bfloat16)
    proj = jnp.einsum(
        "td,dce->tce", first_in, attn_proj, preferred_element_type=jnp.float32
    ).astype(jnp.bfloat16)
    head_grid = proj.reshape(IMG_DEV, SEQ, 3, heads_here, HEAD)
    queries = head_grid[:, :, 0]
    key_heads = head_grid[:, :, 1]
    value_heads = head_grid[:, :, 2]
    raw = (
        jnp.einsum("bqhe,bkhe->bhqk", queries, key_heads, preferred_element_type=jnp.float32)
        * score_scale
    )
    row_top = jnp.max(raw, axis=-1)
    log_total = row_top + jnp.log(jnp.sum(jnp.exp(raw - row_top[..., None]), axis=-1))
    attn_probs = jnp.exp(raw - log_total[..., None]).astype(jnp.bfloat16)
    heads_out = jnp.einsum(
        "bhqk,bkhe->bqhe", attn_probs, value_heads, preferred_element_type=jnp.float32
    )
    heads_out = heads_out.astype(jnp.bfloat16).reshape(tokens, local_width)
    merge_terms = jnp.dot(heads_out, attn_merge, preferred_element_type=jnp.float32)
    middle = wide_input + lax.psum(merge_terms.astype(jnp.bfloat16), "tensor").astype(jnp.float32)
    normed_two, inverse_two = norm_parts(middle)
    second_in = (normed_two * mixer_gain).astype(jnp.bfloat16)
    logits = jnp.dot(second_in, router_weight, preferred_element_type=jnp.float32)
    labels = jnp.arange(experts, dtype=jnp.int32)
    first_hot = (routes[:, 0:1] == labels[None, :]).astype(jnp.float32)
    second_hot = (routes[:, 1:2] == labels[None, :]).astype(jnp.float32)
    gate_first = jax.nn.sigmoid(jnp.sum(logits * (first_hot - second_hot), axis=1))
    kept = keep_mask.astype(jnp.float32)
    gate_weights = jnp.stack([gate_first, 1.0 - gate_first], axis=1) * kept
    slots = slot_table(routes, keep_mask, experts)
    live_mask = keep_mask > 0
    target = jnp.where(live_mask, routes * capacity + slots, experts * capacity).reshape(-1)
    source = jnp.where(live_mask, routes * capacity + slots, 0)
    send_rows = (
        jnp.zeros((experts * capacity, D), jnp.bfloat16)
        .at[target]
        .set(jnp.repeat(second_in, 2, axis=0), mode="drop")
    )
    arrived = spread_rows(send_rows, experts, capacity)
    pre_act = jnp.dot(arrived, expert_up[0], preferred_element_type=jnp.float32)
    hidden = gelu_value(pre_act).astype(jnp.bfloat16)
    partial_terms = jnp.dot(hidden, expert_down[0], preferred_element_type=jnp.float32)
    expert_rows = return_rows(partial_terms, experts, capacity)
    picked = expert_rows[source] * kept[:, :, None]
    mixed_rows = jnp.sum(gate_weights[:, :, None] * picked, axis=1)
    moe = lax.psum(mixed_rows.astype(jnp.bfloat16), "tensor").astype(jnp.float32)
    block_output = (middle + moe).astype(jnp.bfloat16)
    grad_wide = out_grad.astype(jnp.float32)
    d_rows = (
        (gate_weights[:, :, None] * grad_wide[:, None, :])
        .astype(jnp.bfloat16)
        .reshape(tokens * 2, D)
    )
    d_send = jnp.zeros((experts * capacity, D), jnp.bfloat16).at[target].set(d_rows, mode="drop")
    d_arrived = spread_rows(d_send, experts, capacity)
    d_hidden = lax.dot_general(
        d_arrived, expert_down[0], (((1,), (1,)), ((), ())), preferred_element_type=jnp.float32
    )
    down_local = lax.dot_general(
        hidden, d_arrived, (((0,), (0,)), ((), ())), preferred_element_type=jnp.float32
    )
    d_pre = (d_hidden * gelu_slope(pre_act)).astype(jnp.bfloat16)
    up_local = lax.dot_general(
        arrived, d_pre, (((0,), (0,)), ((), ())), preferred_element_type=jnp.float32
    )
    d_terms = lax.dot_general(
        d_pre, expert_up[0], (((1,), (1,)), ((), ())), preferred_element_type=jnp.float32
    )
    d_back = return_rows(d_terms, experts, capacity)
    d_picked = jnp.sum(d_back[source] * kept[:, :, None], axis=1)
    dots_part = jnp.sum(picked * grad_wide[:, None, :], axis=2)
    d_moe, gate_dots = (
        lax.psum(d_picked.astype(jnp.bfloat16), "tensor").astype(jnp.float32),
        lax.psum(dots_part.astype(jnp.bfloat16), "tensor").astype(jnp.float32),
    )
    d_gates = gate_dots * kept
    d_diff = (d_gates[:, 0] - d_gates[:, 1]) * gate_first * (1.0 - gate_first)
    d_logits = (d_diff[:, None] * (first_hot - second_hot)).astype(jnp.bfloat16)
    router_part = lax.dot_general(
        second_in, d_logits, (((0,), (0,)), ((), ())), preferred_element_type=jnp.float32
    )
    d_second = d_moe + lax.dot_general(
        d_logits, router_weight, (((1,), (1,)), ((), ())), preferred_element_type=jnp.float32
    )
    mixer_part = jnp.sum(d_second * normed_two, axis=0)
    d_middle = grad_wide + norm_back(d_second, normed_two, inverse_two, mixer_gain)
    d_low = d_middle.astype(jnp.bfloat16)
    merge_local = lax.dot_general(
        heads_out, d_low, (((0,), (0,)), ((), ())), preferred_element_type=jnp.float32
    )
    d_heads = lax.dot_general(
        d_low, attn_merge, (((1,), (1,)), ((), ())), preferred_element_type=jnp.float32
    ).astype(jnp.bfloat16)
    d_grid = d_heads.reshape(IMG_DEV, SEQ, heads_here, HEAD)
    out_grid = heads_out.reshape(IMG_DEV, SEQ, heads_here, HEAD)
    delta = jnp.einsum("bqhe,bqhe->bhq", d_grid, out_grid, preferred_element_type=jnp.float32)
    raw_again = (
        jnp.einsum("bqhe,bkhe->bhqk", queries, key_heads, preferred_element_type=jnp.float32)
        * score_scale
    )
    probs_wide = jnp.exp(raw_again - log_total[..., None])
    probs_low = probs_wide.astype(jnp.bfloat16)
    d_probs = jnp.einsum("bqhe,bkhe->bhqk", d_grid, value_heads, preferred_element_type=jnp.float32)
    d_raw = (probs_wide * (d_probs - delta[..., None]) * score_scale).astype(jnp.bfloat16)
    d_queries = jnp.einsum("bhqk,bkhe->bqhe", d_raw, key_heads, preferred_element_type=jnp.float32)
    d_keys = jnp.einsum("bhqk,bqhe->bkhe", d_raw, queries, preferred_element_type=jnp.float32)
    d_values = jnp.einsum("bhqk,bqhe->bkhe", probs_low, d_grid, preferred_element_type=jnp.float32)
    d_proj = (
        jnp.stack([d_queries, d_keys, d_values], axis=2)
        .astype(jnp.bfloat16)
        .reshape(tokens, 3, local_width)
    )
    proj_local = jnp.einsum("td,tce->dce", first_in, d_proj, preferred_element_type=jnp.float32)
    first_terms = jnp.einsum("tce,dce->td", d_proj, attn_proj, preferred_element_type=jnp.float32)
    d_first = lax.psum(first_terms.astype(jnp.bfloat16), "tensor").astype(jnp.float32)
    input_grad = d_middle + norm_back(d_first, normed_one, inverse_one, attn_gain)
    attn_part = jnp.sum(d_first * normed_one, axis=0)
    proj_grad, merge_grad, router_grad, attn_gain_grad, mixer_gain_grad = lax.psum(
        (proj_local, merge_local, router_part, attn_part, mixer_part), "expert"
    )
    return (
        block_output,
        input_grad,
        attn_gain_grad,
        proj_grad,
        merge_grad,
        mixer_gain_grad,
        router_grad,
        up_local[None],
        down_local[None],
    )

MESH = pl.DeviceIdType.MESH
VMEM_LIMIT = 60 * 1024 * 1024


class Net:
    def __init__(self, sizes):
        e = lax.axis_index("expert")
        t = lax.axis_index("tensor")
        self.sizes = sizes
        self.at = [e // sizes[1], e % sizes[1], t // sizes[3], t % sizes[3]]

    def shift(self, rel):
        return [(a + r) % s if r else a for a, r, s in zip(self.at, rel, self.sizes)]

    def ident(self, place):
        return (place[0] * self.sizes[1] + place[1], place[2] * self.sizes[3] + place[3])

    def peers(self, dims):
        found = []
        for d in dims:
            for j in range(1, self.sizes[d]):
                rel = [0, 0, 0, 0]
                rel[d] = j
                found.append(self.ident(self.shift(rel)))
        return found

    def enter(self, dims):
        barrier = pltpu.get_barrier_semaphore()
        near = self.peers(dims)
        for peer in near:
            pl.semaphore_signal(barrier, inc=1, device_id=peer, device_id_type=MESH)
        pl.semaphore_wait(barrier, len(near))


def slot_of(rel, sizes, dims):
    index = 0
    for d in dims:
        index = index * sizes[d] + rel[d] % sizes[d]
    return index


def spread(net, own, out, send, recv, order):
    sizes = net.sizes
    dims = sorted(order)
    sent = []

    def block(rel):
        place = net.shift(rel)
        index = 0
        for d in dims:
            index = index * sizes[d] + place[d]
        return index

    def copy_of(source, rel, d, j):
        there = list(rel)
        there[d] = there[d] - j
        step = [0, 0, 0, 0]
        step[d] = j
        return pltpu.make_async_remote_copy(
            src_ref=source,
            dst_ref=out.at[block(rel)],
            send_sem=send.at[len(sent)],
            recv_sem=recv.at[slot_of(there, sizes, dims)],
            device_id=net.ident(net.shift(step)),
            device_id_type=MESH,
        )

    def forward(source, rel, later):
        for d in later:
            for j in range(1, sizes[d]):
                copy = copy_of(source, rel, d, j)
                copy.start()
                sent.append(copy)

    zero = (0, 0, 0, 0)
    forward(own, zero, order)
    out[block(zero)] = own[...]
    yield
    held = [zero]
    for k, d in enumerate(order):
        fresh = []
        for base in held:
            for j in range(1, sizes[d]):
                rel = list(base)
                rel[d] = j
                here = out.at[block(rel)]
                pltpu.make_async_remote_copy(
                    src_ref=here,
                    dst_ref=here,
                    send_sem=send.at[0],
                    recv_sem=recv.at[slot_of(rel, sizes, dims)],
                    device_id=net.peers([d])[0],
                    device_id_type=MESH,
                ).wait_recv()
                forward(here, rel, order[k + 1 :])
                fresh.append(tuple(rel))
        held = held + fresh
        yield
    for copy in sent:
        copy.wait_send()


def together(steps):
    live = list(steps)
    while live:
        left = []
        for step in live:
            try:
                next(step)
                left.append(step)
            except StopIteration:
                pass
        live = left


def count_of(sizes, order):
    total = 1
    for d in order:
        total *= sizes[d]
    return total


def params(cid):
    return pltpu.CompilerParams(
        collective_id=cid, has_side_effects=True, vmem_limit_bytes=VMEM_LIMIT
    )


def vmem(count):
    return [pl.BlockSpec(memory_space=pltpu.VMEM)] * count


def gather_kernel(sizes, orders, *refs):
    n = len(orders)
    net = Net(sizes)
    net.enter(sorted({d for order in orders for d in order}))
    ins, outs, sems = refs[:n], refs[n : 2 * n], refs[2 * n :]
    together(
        [
            spread(net, ins[i], outs[i], sems[2 * i], sems[2 * i + 1], orders[i])
            for i in range(n)
        ]
    )


def gather_call(sizes, cid, arrays, orders):
    counts = [count_of(sizes, order) for order in orders]
    sems = []
    for count in counts:
        sems += [pltpu.SemaphoreType.DMA((count - 1,)), pltpu.SemaphoreType.DMA((count,))]
    return pl.pallas_call(
        functools.partial(gather_kernel, sizes, orders),
        out_shape=[
            jax.ShapeDtypeStruct((count,) + a.shape, a.dtype) for count, a in zip(counts, arrays)
        ],
        in_specs=vmem(len(arrays)),
        out_specs=vmem(len(arrays)),
        scratch_shapes=sems,
        compiler_params=params(cid),
    )(*arrays)


def scatter_tensor(net, terms, landed, send, recv):
    sizes = net.sizes
    sent = []
    index = 0
    for jx in range(sizes[2]):
        for jc in range(sizes[3]):
            if jx == 0 and jc == 0:
                continue
            place = net.shift((0, 0, jx, jc))
            back = slot_of((0, 0, -jx, -jc), sizes, (2, 3)) - 1
            copy = pltpu.make_async_remote_copy(
                src_ref=terms.at[place[2] * sizes[3] + place[3]],
                dst_ref=landed.at[back],
                send_sem=send.at[index],
                recv_sem=recv.at[back],
                device_id=net.ident(place),
                device_id_type=MESH,
            )
            copy.start()
            sent.append((copy, back))
            index += 1
    return sent


def scatter_finish(net, terms, landed, sent):
    own = net.at[2] * net.sizes[3] + net.at[3]
    total = terms[own].astype(jnp.float32)
    for copy, slot in sent:
        copy.wait()
    for slot in range(len(sent)):
        total = total + landed[slot].astype(jnp.float32)
    return total


def tensor_peers_enter(net, extra, experts=False):
    barrier = pltpu.get_barrier_semaphore()
    near = []
    for jx in range(net.sizes[2]):
        for jc in range(net.sizes[3]):
            if jx or jc:
                near.append(net.ident(net.shift((0, 0, jx, jc))))
    near = near + net.peers(extra)
    if experts:
        for jz in range(net.sizes[0]):
            for jy in range(net.sizes[1]):
                if jz or jy:
                    near.append(net.ident(net.shift((jz, jy, 0, 0))))
    for peer in near:
        pl.semaphore_signal(barrier, inc=1, device_id=peer, device_id_type=MESH)
    pl.semaphore_wait(barrier, len(near))


def front_kernel(sizes, tokens, orders, *refs):
    n = len(orders)
    values, gain, weights, merge = refs[:4]
    ins, rest = refs[4 : 4 + n], refs[4 + n :]
    out, heads, proj, probs, first_in = rest[:5]
    outs, rest = rest[5 : 5 + n], rest[5 + n :]
    terms, landed, send, recv = rest[:4]
    sems = rest[4:]
    net = Net(sizes)
    tensor_peers_enter(net, (0, 1))
    steps = [
        spread(net, ins[i], outs[i], sems[2 * i], sems[2 * i + 1], orders[i]) for i in range(n)
    ]
    for step in steps:
        next(step)
    wide, low = jnp.float32, jnp.bfloat16
    normed, unused = norm_parts(values[...].astype(wide))
    first = (normed * gain[...]).astype(low)
    first_in[...] = first
    proj[...] = jnp.dot(first, weights[...], preferred_element_type=wide).astype(low)
    for step in steps:
        next(step)
    padded, width = values.shape[0], heads.shape[1]
    key_live = lax.broadcasted_iota(jnp.int32, (padded, padded), 1) < tokens
    row_live = lax.broadcasted_iota(jnp.int32, (padded, HEAD), 0) < tokens
    for h in range(width // HEAD):
        queries = proj[:, h * HEAD : (h + 1) * HEAD]
        keys = proj[:, width + h * HEAD : width + (h + 1) * HEAD]
        vals = proj[:, 2 * width + h * HEAD : 2 * width + (h + 1) * HEAD]
        raw = lax.dot_general(
            queries, keys, (((1,), (1,)), ((), ())), preferred_element_type=wide
        ) * (HEAD ** (-0.5))
        raw = jnp.where(key_live, raw, -jnp.inf)
        powers = jnp.exp(raw - jnp.max(raw, axis=-1, keepdims=True))
        shares = powers / jnp.sum(powers, axis=-1, keepdims=True)
        probs[h] = shares
        mixed = jnp.dot(shares.astype(low), vals, preferred_element_type=wide)
        heads[:, h * HEAD : (h + 1) * HEAD] = jnp.where(row_live, mixed, 0.0).astype(low)
    merged = jnp.dot(heads[...], merge[...], preferred_element_type=wide)
    rows = terms.shape[1]
    for b in range(terms.shape[0]):
        terms[b] = merged[b * rows : (b + 1) * rows].astype(low)
    sent = scatter_tensor(net, terms, landed, send, recv)
    for step in steps:
        next(step)
    out[...] = scatter_finish(net, terms, landed, sent)
    together(steps)


def front_call(sizes, cid, tokens, values, gain, weights, merge, arrays, orders):
    tensor = sizes[2] * sizes[3]
    padded, width = values.shape
    rows = padded // tensor
    counts = [count_of(sizes, order) for order in orders]
    local = merge.shape[0]
    low = jnp.bfloat16
    dma = pltpu.SemaphoreType.DMA
    sems = []
    for count in counts:
        sems += [dma((count - 1,)), dma((count,))]
    return pl.pallas_call(
        functools.partial(front_kernel, sizes, tokens, orders),
        out_shape=[
            jax.ShapeDtypeStruct((rows, width), jnp.float32),
            jax.ShapeDtypeStruct((padded, local), low),
            jax.ShapeDtypeStruct((padded, 3 * local), low),
            jax.ShapeDtypeStruct((local // HEAD, padded, padded), jnp.float32),
            jax.ShapeDtypeStruct((padded, width), low),
        ]
        + [jax.ShapeDtypeStruct((count,) + a.shape, a.dtype) for count, a in zip(counts, arrays)],
        in_specs=vmem(4 + len(arrays)),
        out_specs=vmem(5 + len(arrays)),
        scratch_shapes=[
            pltpu.VMEM((tensor, rows, width), low),
            pltpu.VMEM((tensor - 1, rows, width), low),
            dma((tensor - 1,)),
            dma((tensor - 1,)),
        ]
        + sems,
        compiler_params=params(cid),
    )(values, gain, weights, merge, *arrays)


def fold(net, part, out, core_in, core_sum, mid_in, mid_sum, low_in, low_sum, z_in, sems, x_first):
    z, y, x, c = net.at
    depth = net.sizes[0]
    kind = part.dtype
    wide = jnp.float32
    core_peer = net.peers([3])[0]
    first_dim, second_dim = (2, 1) if x_first else (1, 2)
    mid_peer, low_peer = net.peers([first_dim])[0], net.peers([second_dim])[0]
    first_at, second_at = net.at[first_dim], net.at[second_dim]

    def remote(source, target, stage, index, landing, peer):
        return pltpu.make_async_remote_copy(
            src_ref=source,
            dst_ref=target,
            send_sem=sems.at[stage, 0, index],
            recv_sem=sems.at[stage, 1, landing],
            device_id=peer,
            device_id_type=MESH,
        )

    zs = [(z + 1 + k) % depth if k < depth - 1 else z for k in range(depth)]
    core, mid, low, far = [], [], [], []
    for k in range(depth):
        copy = remote(part.at[zs[k], :, :, 1 - c], core_in.at[k], 0, k, k, core_peer)
        copy.start()
        core.append(copy)
    yield
    for k in range(depth):
        core[k].wait_recv()
        core_sum[k] = (part[zs[k], :, :, c].astype(wide) + core_in[k].astype(wide)).astype(kind)
        away = core_sum.at[k, :, 1 - first_at] if x_first else core_sum.at[k, 1 - first_at]
        copy = remote(away, mid_in.at[k], 1, k, k, mid_peer)
        copy.start()
        mid.append(copy)
    yield
    for k in range(depth):
        mid[k].wait_recv()
        near = core_sum[k, :, first_at] if x_first else core_sum[k, first_at]
        mid_sum[k] = (near.astype(wide) + mid_in[k].astype(wide)).astype(kind)
        copy = remote(mid_sum.at[k, 1 - second_at], low_in.at[k], 2, k, k, low_peer)
        copy.start()
        low.append(copy)
    yield
    for k in range(depth):
        low[k].wait_recv()
        total = mid_sum[k, second_at].astype(wide) + low_in[k].astype(wide)
        if k == depth - 1:
            out[...] = total
        else:
            low_sum[k] = total.astype(kind)
            landing = depth - k - 2
            peer = net.ident([zs[k], y, x, c])
            copy = remote(low_sum.at[k], z_in.at[landing], 3, k, landing, peer)
            copy.start()
            far.append(copy)
    yield
    for k in range(depth - 1):
        far[k].wait_recv()
    total = out[...]
    for k in range(depth - 1):
        total = total + z_in[k].astype(wide)
    out[...] = total
    for copy in core + mid + low + far:
        copy.wait_send()


def fold_scratch(sizes, shape, kind):
    depth, ys, xs, cs = sizes
    return [
        pltpu.VMEM((depth, ys, xs) + shape, kind),
        pltpu.VMEM((depth, ys, xs) + shape, kind),
        pltpu.VMEM((depth, 2) + shape, kind),
        pltpu.VMEM((depth, 2) + shape, kind),
        pltpu.VMEM((depth,) + shape, kind),
        pltpu.VMEM((depth - 1,) + shape, kind),
        pltpu.VMEM((depth - 1,) + shape, kind),
        pltpu.SemaphoreType.DMA((4, 2, depth)),
    ]


def fold_kernel(sizes, firsts, *refs):
    n = len(firsts)
    net = Net(sizes)
    net.enter((0, 1, 2, 3))
    ins, outs, rest = refs[:n], refs[n : 2 * n], refs[2 * n :]
    together(
        [
            fold(net, ins[i], outs[i], *rest[8 * i : 8 * i + 8], firsts[i])
            for i in range(n)
        ]
    )


def fold_call(sizes, cid, arrays, firsts):
    shaped = [a.reshape(tuple(sizes) + a.shape[1:]) for a in arrays]
    scratch = []
    for a in arrays:
        scratch += fold_scratch(sizes, a.shape[1:], a.dtype)
    return pl.pallas_call(
        functools.partial(fold_kernel, sizes, firsts),
        out_shape=[jax.ShapeDtypeStruct(a.shape[1:], jnp.float32) for a in arrays],
        in_specs=vmem(len(arrays)),
        out_specs=vmem(len(arrays)),
        scratch_shapes=scratch,
        compiler_params=params(cid),
    )(*shaped)


def ring(net, part, y_in, y_sum, z_in, total, own, out, sems, send, recv):
    z, y, x, c = net.at
    depth = net.sizes[0]
    kind = part.dtype
    wide = jnp.float32
    y_peer = net.peers([1])[0]
    zs = [(z + 1 + k) % depth if k < depth - 1 else z for k in range(depth)]
    near, far = [], []

    def remote(source, target, stage, index, landing, peer):
        return pltpu.make_async_remote_copy(
            src_ref=source,
            dst_ref=target,
            send_sem=sems.at[stage, 0, index],
            recv_sem=sems.at[stage, 1, landing],
            device_id=peer,
            device_id_type=MESH,
        )

    for k in range(depth):
        copy = remote(part.at[zs[k], 1 - y], y_in.at[k], 0, k, k, y_peer)
        copy.start()
        near.append(copy)
    yield
    for k in range(depth):
        near[k].wait_recv()
        here = part[zs[k], y].astype(wide) + y_in[k].astype(wide)
        if k == depth - 1:
            total[...] = here
        else:
            y_sum[k] = here.astype(kind)
            landing = depth - k - 2
            peer = net.ident([zs[k], y, x, c])
            copy = remote(y_sum.at[k], z_in.at[landing], 1, k, landing, peer)
            copy.start()
            far.append(copy)
    yield
    for k in range(depth - 1):
        far[k].wait_recv()
    done = total[...]
    for k in range(depth - 1):
        done = done + z_in[k].astype(wide)
    own[...] = done.astype(kind)
    yield
    yield from spread(net, own, out, send, recv, (0, 1))
    for copy in near + far:
        copy.wait_send()


def ring_scratch(sizes, shape, kind):
    depth = sizes[0]
    count = depth * sizes[1]
    return [
        pltpu.VMEM((depth,) + shape, kind),
        pltpu.VMEM((depth - 1,) + shape, kind),
        pltpu.VMEM((depth - 1,) + shape, kind),
        pltpu.VMEM(shape, jnp.float32),
        pltpu.VMEM(shape, kind),
        pltpu.SemaphoreType.DMA((2, 2, depth)),
        pltpu.SemaphoreType.DMA((count - 1,)),
        pltpu.SemaphoreType.DMA((count,)),
    ]


def tail_kernel(sizes, gain_row, *refs):
    terms, d_middle, normed, inverse, gain, small, proj, merge = refs[:8]
    grad_all, proj_all, merge_all, small_out = refs[8:12]
    rest = refs[12:]
    landed, grad_own, small_in, small_sum, sc_send, sc_recv, g_send, g_recv, s_send, s_recv = rest[
        :10
    ]
    ring_one, ring_two = rest[10:18], rest[18:26]
    net = Net(sizes)
    tensor_peers_enter(net, (), True)
    sent = scatter_tensor(net, terms, landed, sc_send, sc_recv)
    rings = [
        ring(net, proj, *ring_one[:5], proj_all, *ring_one[5:]),
        ring(net, merge, *ring_two[:5], merge_all, *ring_two[5:]),
    ]
    for step in rings:
        next(step)
    for step in rings:
        next(step)
    d_first = scatter_finish(net, terms, landed, sent)
    scaled = d_first * gain[...]
    plain = normed[...]
    mean = jnp.mean(scaled, axis=-1, keepdims=True)
    mixed = jnp.mean(scaled * plain, axis=-1, keepdims=True)
    grad = d_middle[...] + inverse[...] * (scaled - mean - plain * mixed)
    grad_own[...] = grad.astype(jnp.bfloat16)
    part = jnp.sum(d_first * plain, axis=0, keepdims=True)
    row = lax.broadcasted_iota(jnp.int32, small.shape, 0)
    small_sum[0] = jnp.where(row == gain_row, part, small[...])
    copies = []

    def exchange(stage, slot, landing, place):
        copy = pltpu.make_async_remote_copy(
            src_ref=small_sum.at[stage],
            dst_ref=small_in.at[landing],
            send_sem=s_send.at[slot],
            recv_sem=s_recv.at[landing],
            device_id=net.ident(place),
            device_id_type=MESH,
        )
        copy.start()
        copies.append(copy)
        return copy

    exchange(0, 0, 0, net.shift((0, 0, 0, 1))).wait_recv()
    small_sum[1] = small_sum[0] + small_in[0]
    exchange(1, 1, 1, net.shift((0, 0, 1, 0))).wait_recv()
    small_sum[2] = small_sum[1] + small_in[1]
    grad_step = spread(net, grad_own, grad_all, g_send, g_recv, (2, 3))
    next(grad_step)
    slot = 2
    final = []
    for jz in range(sizes[0]):
        for jy in range(sizes[1]):
            if jz or jy:
                landing = 1 + slot_of((-jz, -jy, 0, 0), sizes, (0, 1))
                final.append(exchange(2, slot, landing, net.shift((jz, jy, 0, 0))))
                slot += 1
    for step in rings:
        next(step)
    for step in rings:
        next(step)
    next(grad_step)
    for step in rings:
        next(step)
    for copy in final:
        copy.wait_recv()
    total = small_sum[2]
    for k in range(len(final)):
        total = total + small_in[2 + k]
    small_out[...] = total
    for copy in copies:
        copy.wait_send()
    together([grad_step] + rings)


def tail_call(sizes, cid, gain_row, terms, d_middle, normed, inverse, gain, small, proj, merge):
    experts_axis, tensor = sizes[0] * sizes[1], sizes[2] * sizes[3]
    steps = 1 + experts_axis
    dma = pltpu.SemaphoreType.DMA
    shape = d_middle.shape
    low = jnp.bfloat16
    split = tuple(sizes[:2])
    proj = proj.reshape(split + (proj.shape[0] // experts_axis,) + proj.shape[1:])
    merge = merge.reshape(split + (merge.shape[0] // experts_axis,) + merge.shape[1:])
    return pl.pallas_call(
        functools.partial(tail_kernel, sizes, gain_row),
        out_shape=[
            jax.ShapeDtypeStruct((tensor,) + shape, low),
            jax.ShapeDtypeStruct((experts_axis,) + proj.shape[2:], low),
            jax.ShapeDtypeStruct((experts_axis,) + merge.shape[2:], low),
            jax.ShapeDtypeStruct(small.shape, jnp.float32),
        ],
        in_specs=vmem(8),
        out_specs=vmem(4),
        scratch_shapes=[
            pltpu.VMEM((tensor - 1,) + shape, low),
            pltpu.VMEM(shape, low),
            pltpu.VMEM((steps,) + small.shape, jnp.float32),
            pltpu.VMEM((3,) + small.shape, jnp.float32),
            dma((tensor - 1,)),
            dma((tensor - 1,)),
            dma((tensor - 1,)),
            dma((tensor,)),
            dma((steps,)),
            dma((steps,)),
        ]
        + ring_scratch(sizes, proj.shape[2:], low)
        + ring_scratch(sizes, merge.shape[2:], low),
        compiler_params=params(cid),
    )(terms, d_middle, normed, inverse, gain, small, proj, merge)


def on_device_dense(
    sizes,
    block_input,
    attn_gain,
    attn_proj,
    attn_merge,
    mixer_gain,
    router_weight,
    expert_up,
    expert_down,
    routes,
    keep_mask,
    out_grad,
):
    experts_axis, tensor = sizes[0] * sizes[1], sizes[2] * sizes[3]
    experts = experts_axis // PAIR
    tokens = block_input.shape[0]
    rows = -(-(-(-tokens // tensor)) // 8) * 8
    padded = rows * tensor
    local_width = attn_proj.shape[2]
    heads_here = local_width // HEAD
    score_scale = HEAD ** (-0.5)
    start = lax.axis_index("tensor") * rows
    low = jnp.bfloat16
    wide = jnp.float32

    def fill(array):
        return jnp.pad(array, ((0, padded - tokens), (0, 0)))

    def quarter(array):
        return lax.dynamic_slice_in_dim(array, start, rows, axis=0)

    input_q = quarter(fill(block_input)).astype(wide)
    grad_q_low = quarter(fill(out_grad))
    grad_q = grad_q_low.astype(wide)
    route_q = quarter(fill(routes))
    keep_q = quarter(fill(keep_mask))

    normed_q, inverse_q = norm_parts(input_q)
    codes = jnp.concatenate([route_q, keep_q], axis=1).astype(wide).T
    codes = jnp.pad(codes, ((0, 4), (0, -rows % 128)))
    flat_proj = attn_proj.reshape(D, 3 * local_width)
    merged, heads_out, proj, probs_wide, first_in, grad_all, codes_all = front_call(
        sizes,
        1,
        tokens,
        fill(block_input),
        attn_gain[None, :],
        flat_proj,
        attn_merge,
        [grad_q_low, codes],
        [(0, 2, 1, 3), (0, 1, 2, 3)],
    )
    head_grid = proj.reshape(padded, 3, heads_here, HEAD)
    queries, key_heads, value_heads = head_grid[:, 0], head_grid[:, 1], head_grid[:, 2]
    probs_low = probs_wide.astype(low)
    middle = input_q + merged
    normed_two, inverse_two = norm_parts(middle)
    second_q = (normed_two * mixer_gain).astype(low)

    (second_all,) = gather_call(sizes, 2, [second_q], [(0, 1, 2, 3)])
    total = experts_axis * padded
    arrived = second_all.reshape(total, D)
    grads = grad_all.reshape(total, D)

    label = lax.axis_index("expert") // PAIR
    code = codes_all[:, :4, :rows].transpose(0, 2, 1).reshape(total, 4)
    labels = jnp.arange(experts, dtype=wide)
    pick_all = (code[:, 0:1] == labels).astype(wide) - (code[:, 1:2] == labels).astype(wide)
    logits_all = jnp.dot(arrived, router_weight, preferred_element_type=wide)
    gate_all = jax.nn.sigmoid(jnp.sum(logits_all * pick_all, axis=1, keepdims=True))
    live_first = jnp.where(code[:, 0:1] == label.astype(wide), code[:, 2:3], 0.0)
    live_second = jnp.where(code[:, 1:2] == label.astype(wide), code[:, 3:4], 0.0)
    weight = live_first * gate_all + live_second * (1.0 - gate_all)
    side = live_first - live_second

    up, down = expert_up[0], expert_down[0]
    pre_act = jnp.dot(arrived, up, preferred_element_type=wide)
    hidden = gelu_value(pre_act).astype(low)
    partial_terms = jnp.dot(hidden, down, preferred_element_type=wide)
    moe_terms = (weight * partial_terms).astype(low)
    dots = jnp.sum(
        (partial_terms * grads.astype(wide)).reshape(experts_axis * tensor, rows, D), axis=2
    ) * side.reshape(experts_axis * tensor, rows)
    dots = jnp.broadcast_to(
        jnp.pad(dots, ((0, 0), (0, -rows % 128)))[:, None, :],
        (experts_axis * tensor, 8, -(-rows // 128) * 128),
    )
    d_rows = (weight * grads.astype(wide)).astype(low)
    d_hidden = lax.dot_general(d_rows, down, (((1,), (1,)), ((), ())), preferred_element_type=wide)
    down_local = lax.dot_general(
        hidden, d_rows, (((0,), (0,)), ((), ())), preferred_element_type=wide
    )
    d_pre = (d_hidden * gelu_slope(pre_act)).astype(low)
    up_local = lax.dot_general(arrived, d_pre, (((0,), (0,)), ((), ())), preferred_element_type=wide)
    d_terms = lax.dot_general(
        d_pre, up, (((1,), (1,)), ((), ())), preferred_element_type=wide
    ).astype(low)

    shape = (experts_axis * tensor, rows, D)
    moe, d_moe, dots_sum = fold_call(
        sizes,
        3,
        [moe_terms.reshape(shape), d_terms.reshape(shape), dots],
        (True, False, True),
    )
    block_q = (middle + moe).astype(low)
    mine = jnp.arange(experts, dtype=jnp.int32)
    pick = (route_q[:, 0:1] == mine).astype(wide) - (route_q[:, 1:2] == mine).astype(wide)
    logits = jnp.dot(second_q, router_weight, preferred_element_type=wide)
    gate_first = jax.nn.sigmoid(jnp.sum(logits * pick, axis=1))
    d_diff = dots_sum[0, :rows] * gate_first * (1.0 - gate_first)
    d_logits = (d_diff[:, None] * pick).astype(low)
    router_part = lax.dot_general(
        d_logits, second_q, (((0,), (0,)), ((), ())), preferred_element_type=wide
    )
    d_second = d_moe + lax.dot_general(
        d_logits, router_weight, (((1,), (1,)), ((), ())), preferred_element_type=wide
    )
    mixer_part = jnp.sum(d_second * normed_two, axis=0, keepdims=True)
    d_middle = grad_q + norm_back(d_second, normed_two, inverse_two, mixer_gain)
    d_low_q = d_middle.astype(low)

    low_rows, block_rows = gather_call(sizes, 4, [d_low_q, block_q], [(2, 3), (2, 3)])
    d_low = low_rows.reshape(padded, D)
    block_output = block_rows.reshape(padded, D)[:tokens]

    d_heads = lax.dot_general(
        d_low, attn_merge, (((1,), (1,)), ((), ())), preferred_element_type=wide
    ).astype(low)
    d_grid = d_heads.reshape(padded, heads_here, HEAD)
    out_grid = heads_out.reshape(padded, heads_here, HEAD)
    delta = jnp.sum(d_grid.astype(wide) * out_grid.astype(wide), axis=2).T
    d_probs = jnp.einsum("qhe,khe->hqk", d_grid, value_heads, preferred_element_type=wide)
    d_raw = (probs_wide * (d_probs - delta[..., None]) * score_scale).astype(low)
    d_queries = jnp.einsum("hqk,khe->qhe", d_raw, key_heads, preferred_element_type=wide)
    d_keys = jnp.einsum("hqk,qhe->khe", d_raw, queries, preferred_element_type=wide)
    d_values = jnp.einsum("hqk,qhe->khe", probs_low, d_grid, preferred_element_type=wide)
    d_proj = jnp.concatenate(
        [part.astype(low).reshape(padded, local_width) for part in (d_queries, d_keys, d_values)],
        axis=1,
    )
    first_terms = lax.dot_general(
        d_proj, flat_proj, (((1,), (1,)), ((), ())), preferred_element_type=wide
    ).astype(low)
    small = jnp.concatenate([router_part, mixer_part], axis=0)
    small = jnp.pad(small, ((0, 1 + -(experts + 2) % 8), (0, 0)))
    proj_local = lax.dot_general(
        first_in, d_proj, (((0,), (0,)), ((), ())), preferred_element_type=wide
    ).astype(low)
    merge_local = lax.dot_general(
        heads_out, d_low, (((0,), (0,)), ((), ())), preferred_element_type=wide
    ).astype(low)
    grad_rows, proj_all, merge_all, small_all = tail_call(
        sizes,
        5,
        experts + 1,
        first_terms.reshape(tensor, rows, D),
        d_middle,
        normed_q,
        inverse_q,
        attn_gain[None, :],
        small,
        proj_local,
        merge_local,
    )
    input_grad = grad_rows.reshape(padded, D)[:tokens].astype(wide)
    proj_grad = proj_all.astype(wide).reshape(D, 3, local_width)
    merge_grad = merge_all.astype(wide).reshape(local_width, D)
    return (
        block_output,
        input_grad,
        small_all[experts + 1],
        proj_grad,
        merge_grad,
        small_all[experts],
        small_all[:experts].T,
        up_local[None],
        down_local[None],
    )


def program_of(mesh):
    experts_axis, tensor = mesh.shape["expert"], mesh.shape["tensor"]
    if tensor != 4 or experts_axis % 2 or experts_axis < 4:
        return on_device
    capacity = max(8, 4 * TOK_DEV // (experts_axis // PAIR) // 8 * 8)
    rows = -(-(-(-TOK_DEV // tensor)) // 8) * 8
    if 4 * rows * tensor > 5 * capacity:
        return on_device
    return functools.partial(on_device_dense, (experts_axis // 2, 2, tensor // 2, 2))


def solution(mesh):
    in_specs = (
        P("expert", None),
        P(),
        P(None, None, "tensor"),
        P("tensor", None),
        P(),
        P(),
        P("expert", None, "tensor"),
        P("expert", "tensor", None),
        P("expert", None),
        P("expert", None),
        P("expert", None),
    )
    out_specs = (
        P("expert", None),
        P("expert", None),
        P(),
        P(None, None, "tensor"),
        P("tensor", None),
        P(),
        P(),
        P("expert", None, "tensor"),
        P("expert", "tensor", None),
    )
    return jax.shard_map(
        program_of(mesh), mesh=mesh, in_specs=in_specs, out_specs=out_specs, check_vma=False
    )
```

```python
import functools

import jax
import jax.numpy as jnp
from jax import lax
from jax.experimental import pallas as pl
from jax.experimental.pallas import tpu as pltpu
from jax.sharding import PartitionSpec as P

D = 768
SEQ = 197
PAIR = 2
IMG_DEV = 1
HEAD = 64
TOK_DEV = 197


EPS = 1e-06
ROOT_HALF = 0.7071067811865476
INV_ROOT_TAU = 0.3989422804014327


def norm_parts(values):
    center = values - jnp.mean(values, axis=-1, keepdims=True)
    inverse = lax.rsqrt(jnp.mean(center * center, axis=-1, keepdims=True) + EPS)
    return (center * inverse, inverse)


def norm_back(upstream, normed, inverse, gain):
    scaled = upstream * gain
    return inverse * (
        scaled
        - jnp.mean(scaled, axis=-1, keepdims=True)
        - normed * jnp.mean(scaled * normed, axis=-1, keepdims=True)
    )


def gelu_value(pre_act):
    return 0.5 * pre_act * (1.0 + lax.erf(pre_act * ROOT_HALF))


def gelu_slope(pre_act):
    return (
        0.5 * (1.0 + lax.erf(pre_act * ROOT_HALF))
        + pre_act * jnp.exp(-0.5 * pre_act * pre_act) * INV_ROOT_TAU
    )


def slot_table(routes, keep_mask, experts):
    labels = jnp.arange(experts, dtype=jnp.int32)
    chosen = routes[:, :, None] == labels[None, None, :]
    hits = jnp.where(chosen & (keep_mask[:, :, None] > 0), 1, 0).astype(jnp.int32)
    per_token = jnp.sum(hits, axis=1)
    before = jnp.cumsum(per_token, axis=0) - per_token
    return jnp.sum(jnp.where(chosen, before[:, None, :], 0), axis=2)


def spread_rows(slot_rows, experts, capacity):
    width = slot_rows.shape[-1]
    paired = jnp.broadcast_to(
        slot_rows.reshape(experts, 1, capacity, width), (experts, PAIR, capacity, width)
    )
    paired = paired.reshape(experts * PAIR, capacity, width)
    arrived = lax.all_to_all(paired, "expert", split_axis=0, concat_axis=0, tiled=True)
    return arrived.reshape(-1, width)


def return_rows(partial_terms, experts, capacity):
    width = partial_terms.shape[-1]
    sent_rows = partial_terms.astype(jnp.bfloat16).reshape(experts * PAIR, capacity, width)
    landed = lax.all_to_all(sent_rows, "expert", split_axis=0, concat_axis=0, tiled=True).astype(
        jnp.float32
    )
    return jnp.sum(landed.reshape(experts, PAIR, capacity, width), axis=1).reshape(
        experts * capacity, width
    )


def on_device(
    block_input,
    attn_gain,
    attn_proj,
    attn_merge,
    mixer_gain,
    router_weight,
    expert_up,
    expert_down,
    routes,
    keep_mask,
    out_grad,
):
    experts = lax.axis_size("expert") // PAIR
    capacity = max(8, 4 * TOK_DEV // experts // 8 * 8)
    local_width = attn_proj.shape[2]
    heads_here = local_width // HEAD
    score_scale = HEAD ** (-0.5)
    tokens = block_input.shape[0]
    wide_input = block_input.astype(jnp.float32)
    normed_one, inverse_one = norm_parts(wide_input)
    first_in = (normed_one * attn_gain).astype(jnp.bfloat16)
    proj = jnp.einsum(
        "td,dce->tce", first_in, attn_proj, preferred_element_type=jnp.float32
    ).astype(jnp.bfloat16)
    head_grid = proj.reshape(IMG_DEV, SEQ, 3, heads_here, HEAD)
    queries = head_grid[:, :, 0]
    key_heads = head_grid[:, :, 1]
    value_heads = head_grid[:, :, 2]
    raw = (
        jnp.einsum("bqhe,bkhe->bhqk", queries, key_heads, preferred_element_type=jnp.float32)
        * score_scale
    )
    row_top = jnp.max(raw, axis=-1)
    log_total = row_top + jnp.log(jnp.sum(jnp.exp(raw - row_top[..., None]), axis=-1))
    attn_probs = jnp.exp(raw - log_total[..., None]).astype(jnp.bfloat16)
    heads_out = jnp.einsum(
        "bhqk,bkhe->bqhe", attn_probs, value_heads, preferred_element_type=jnp.float32
    )
    heads_out = heads_out.astype(jnp.bfloat16).reshape(tokens, local_width)
    merge_terms = jnp.dot(heads_out, attn_merge, preferred_element_type=jnp.float32)
    middle = wide_input + lax.psum(merge_terms.astype(jnp.bfloat16), "tensor").astype(jnp.float32)
    normed_two, inverse_two = norm_parts(middle)
    second_in = (normed_two * mixer_gain).astype(jnp.bfloat16)
    logits = jnp.dot(second_in, router_weight, preferred_element_type=jnp.float32)
    labels = jnp.arange(experts, dtype=jnp.int32)
    first_hot = (routes[:, 0:1] == labels[None, :]).astype(jnp.float32)
    second_hot = (routes[:, 1:2] == labels[None, :]).astype(jnp.float32)
    gate_first = jax.nn.sigmoid(jnp.sum(logits * (first_hot - second_hot), axis=1))
    kept = keep_mask.astype(jnp.float32)
    gate_weights = jnp.stack([gate_first, 1.0 - gate_first], axis=1) * kept
    slots = slot_table(routes, keep_mask, experts)
    live_mask = keep_mask > 0
    target = jnp.where(live_mask, routes * capacity + slots, experts * capacity).reshape(-1)
    source = jnp.where(live_mask, routes * capacity + slots, 0)
    send_rows = (
        jnp.zeros((experts * capacity, D), jnp.bfloat16)
        .at[target]
        .set(jnp.repeat(second_in, 2, axis=0), mode="drop")
    )
    arrived = spread_rows(send_rows, experts, capacity)
    pre_act = jnp.dot(arrived, expert_up[0], preferred_element_type=jnp.float32)
    hidden = gelu_value(pre_act).astype(jnp.bfloat16)
    partial_terms = jnp.dot(hidden, expert_down[0], preferred_element_type=jnp.float32)
    expert_rows = return_rows(partial_terms, experts, capacity)
    picked = expert_rows[source] * kept[:, :, None]
    mixed_rows = jnp.sum(gate_weights[:, :, None] * picked, axis=1)
    moe = lax.psum(mixed_rows.astype(jnp.bfloat16), "tensor").astype(jnp.float32)
    block_output = (middle + moe).astype(jnp.bfloat16)
    grad_wide = out_grad.astype(jnp.float32)
    d_rows = (
        (gate_weights[:, :, None] * grad_wide[:, None, :])
        .astype(jnp.bfloat16)
        .reshape(tokens * 2, D)
    )
    d_send = jnp.zeros((experts * capacity, D), jnp.bfloat16).at[target].set(d_rows, mode="drop")
    d_arrived = spread_rows(d_send, experts, capacity)
    d_hidden = lax.dot_general(
        d_arrived, expert_down[0], (((1,), (1,)), ((), ())), preferred_element_type=jnp.float32
    )
    down_local = lax.dot_general(
        hidden, d_arrived, (((0,), (0,)), ((), ())), preferred_element_type=jnp.float32
    )
    d_pre = (d_hidden * gelu_slope(pre_act)).astype(jnp.bfloat16)
    up_local = lax.dot_general(
        arrived, d_pre, (((0,), (0,)), ((), ())), preferred_element_type=jnp.float32
    )
    d_terms = lax.dot_general(
        d_pre, expert_up[0], (((1,), (1,)), ((), ())), preferred_element_type=jnp.float32
    )
    d_back = return_rows(d_terms, experts, capacity)
    d_picked = jnp.sum(d_back[source] * kept[:, :, None], axis=1)
    dots_part = jnp.sum(picked * grad_wide[:, None, :], axis=2)
    d_moe, gate_dots = (
        lax.psum(d_picked.astype(jnp.bfloat16), "tensor").astype(jnp.float32),
        lax.psum(dots_part.astype(jnp.bfloat16), "tensor").astype(jnp.float32),
    )
    d_gates = gate_dots * kept
    d_diff = (d_gates[:, 0] - d_gates[:, 1]) * gate_first * (1.0 - gate_first)
    d_logits = (d_diff[:, None] * (first_hot - second_hot)).astype(jnp.bfloat16)
    router_part = lax.dot_general(
        second_in, d_logits, (((0,), (0,)), ((), ())), preferred_element_type=jnp.float32
    )
    d_second = d_moe + lax.dot_general(
        d_logits, router_weight, (((1,), (1,)), ((), ())), preferred_element_type=jnp.float32
    )
    mixer_part = jnp.sum(d_second * normed_two, axis=0)
    d_middle = grad_wide + norm_back(d_second, normed_two, inverse_two, mixer_gain)
    d_low = d_middle.astype(jnp.bfloat16)
    merge_local = lax.dot_general(
        heads_out, d_low, (((0,), (0,)), ((), ())), preferred_element_type=jnp.float32
    )
    d_heads = lax.dot_general(
        d_low, attn_merge, (((1,), (1,)), ((), ())), preferred_element_type=jnp.float32
    ).astype(jnp.bfloat16)
    d_grid = d_heads.reshape(IMG_DEV, SEQ, heads_here, HEAD)
    out_grid = heads_out.reshape(IMG_DEV, SEQ, heads_here, HEAD)
    delta = jnp.einsum("bqhe,bqhe->bhq", d_grid, out_grid, preferred_element_type=jnp.float32)
    raw_again = (
        jnp.einsum("bqhe,bkhe->bhqk", queries, key_heads, preferred_element_type=jnp.float32)
        * score_scale
    )
    probs_wide = jnp.exp(raw_again - log_total[..., None])
    probs_low = probs_wide.astype(jnp.bfloat16)
    d_probs = jnp.einsum("bqhe,bkhe->bhqk", d_grid, value_heads, preferred_element_type=jnp.float32)
    d_raw = (probs_wide * (d_probs - delta[..., None]) * score_scale).astype(jnp.bfloat16)
    d_queries = jnp.einsum("bhqk,bkhe->bqhe", d_raw, key_heads, preferred_element_type=jnp.float32)
    d_keys = jnp.einsum("bhqk,bqhe->bkhe", d_raw, queries, preferred_element_type=jnp.float32)
    d_values = jnp.einsum("bhqk,bqhe->bkhe", probs_low, d_grid, preferred_element_type=jnp.float32)
    d_proj = (
        jnp.stack([d_queries, d_keys, d_values], axis=2)
        .astype(jnp.bfloat16)
        .reshape(tokens, 3, local_width)
    )
    proj_local = jnp.einsum("td,tce->dce", first_in, d_proj, preferred_element_type=jnp.float32)
    first_terms = jnp.einsum("tce,dce->td", d_proj, attn_proj, preferred_element_type=jnp.float32)
    d_first = lax.psum(first_terms.astype(jnp.bfloat16), "tensor").astype(jnp.float32)
    input_grad = d_middle + norm_back(d_first, normed_one, inverse_one, attn_gain)
    attn_part = jnp.sum(d_first * normed_one, axis=0)
    proj_grad, merge_grad, router_grad, attn_gain_grad, mixer_gain_grad = lax.psum(
        (proj_local, merge_local, router_part, attn_part, mixer_part), "expert"
    )
    return (
        block_output,
        input_grad,
        attn_gain_grad,
        proj_grad,
        merge_grad,
        mixer_gain_grad,
        router_grad,
        up_local[None],
        down_local[None],
    )

MESH = pl.DeviceIdType.MESH
VMEM_LIMIT = 60 * 1024 * 1024


class Net:
    def __init__(self, sizes):
        e = lax.axis_index("expert")
        t = lax.axis_index("tensor")
        self.sizes = sizes
        self.at = [e // sizes[1], e % sizes[1], t // sizes[3], t % sizes[3]]

    def shift(self, rel):
        return [(a + r) % s if r else a for a, r, s in zip(self.at, rel, self.sizes)]

    def ident(self, place):
        return (place[0] * self.sizes[1] + place[1], place[2] * self.sizes[3] + place[3])

    def peers(self, dims):
        found = []
        for d in dims:
            for j in range(1, self.sizes[d]):
                rel = [0, 0, 0, 0]
                rel[d] = j
                found.append(self.ident(self.shift(rel)))
        return found

    def enter(self, dims):
        barrier = pltpu.get_barrier_semaphore()
        near = self.peers(dims)
        for peer in near:
            pl.semaphore_signal(barrier, inc=1, device_id=peer, device_id_type=MESH)
        pl.semaphore_wait(barrier, len(near))


def slot_of(rel, sizes, dims):
    index = 0
    for d in dims:
        index = index * sizes[d] + rel[d] % sizes[d]
    return index


def spread(net, own, out, send, recv, order, fine=False):
    sizes = net.sizes
    dims = sorted(order)
    sent = []

    def block(rel):
        place = net.shift(rel)
        index = 0
        for d in dims:
            index = index * sizes[d] + place[d]
        return index

    def copy_of(source, rel, d, j):
        there = list(rel)
        there[d] = there[d] - j
        step = [0, 0, 0, 0]
        step[d] = j
        return pltpu.make_async_remote_copy(
            src_ref=source,
            dst_ref=out.at[block(rel)],
            send_sem=send.at[len(sent)],
            recv_sem=recv.at[slot_of(there, sizes, dims)],
            device_id=net.ident(net.shift(step)),
            device_id_type=MESH,
        )

    def forward(source, rel, later):
        for d in later:
            for j in range(1, sizes[d]):
                copy = copy_of(source, rel, d, j)
                copy.start()
                sent.append(copy)

    zero = (0, 0, 0, 0)
    forward(own, zero, order)
    out[block(zero)] = own[...]
    yield
    held = [zero]
    for k, d in enumerate(order):
        fresh = []
        for base in held:
            for j in range(1, sizes[d]):
                rel = list(base)
                rel[d] = j
                here = out.at[block(rel)]
                pltpu.make_async_remote_copy(
                    src_ref=here,
                    dst_ref=here,
                    send_sem=send.at[0],
                    recv_sem=recv.at[slot_of(rel, sizes, dims)],
                    device_id=net.peers([d])[0],
                    device_id_type=MESH,
                ).wait_recv()
                forward(here, rel, order[k + 1 :])
                fresh.append(tuple(rel))
                if fine:
                    yield
        held = held + fresh
        yield
    for copy in sent:
        copy.wait_send()


def together(steps):
    live = list(steps)
    while live:
        left = []
        for step in live:
            try:
                next(step)
                left.append(step)
            except StopIteration:
                pass
        live = left


def count_of(sizes, order):
    total = 1
    for d in order:
        total *= sizes[d]
    return total


def params(cid):
    return pltpu.CompilerParams(
        collective_id=cid, has_side_effects=True, vmem_limit_bytes=VMEM_LIMIT
    )


def vmem(count):
    return [pl.BlockSpec(memory_space=pltpu.VMEM)] * count


def gather_kernel(sizes, orders, *refs):
    n = len(orders)
    net = Net(sizes)
    net.enter(sorted({d for order in orders for d in order}))
    ins, outs, sems = refs[:n], refs[n : 2 * n], refs[2 * n :]
    together(
        [
            spread(net, ins[i], outs[i], sems[2 * i], sems[2 * i + 1], orders[i], True)
            for i in range(n)
        ]
    )


def gather_call(sizes, cid, arrays, orders):
    counts = [count_of(sizes, order) for order in orders]
    sems = []
    for count in counts:
        sems += [pltpu.SemaphoreType.DMA((count - 1,)), pltpu.SemaphoreType.DMA((count,))]
    return pl.pallas_call(
        functools.partial(gather_kernel, sizes, orders),
        out_shape=[
            jax.ShapeDtypeStruct((count,) + a.shape, a.dtype) for count, a in zip(counts, arrays)
        ],
        in_specs=vmem(len(arrays)),
        out_specs=vmem(len(arrays)),
        scratch_shapes=sems,
        compiler_params=params(cid),
    )(*arrays)


def scatter_tensor(net, terms, landed, send, recv):
    sizes = net.sizes
    sent = []
    index = 0
    for jx in range(sizes[2]):
        for jc in range(sizes[3]):
            if jx == 0 and jc == 0:
                continue
            place = net.shift((0, 0, jx, jc))
            back = slot_of((0, 0, -jx, -jc), sizes, (2, 3)) - 1
            copy = pltpu.make_async_remote_copy(
                src_ref=terms.at[place[2] * sizes[3] + place[3]],
                dst_ref=landed.at[back],
                send_sem=send.at[index],
                recv_sem=recv.at[back],
                device_id=net.ident(place),
                device_id_type=MESH,
            )
            copy.start()
            sent.append((copy, back))
            index += 1
    return sent


def scatter_finish(net, terms, landed, sent):
    own = net.at[2] * net.sizes[3] + net.at[3]
    total = terms[own].astype(jnp.float32)
    for copy, slot in sent:
        copy.wait()
    for slot in range(len(sent)):
        total = total + landed[slot].astype(jnp.float32)
    return total


def tensor_peers_enter(net, extra, experts=False):
    barrier = pltpu.get_barrier_semaphore()
    near = []
    for jx in range(net.sizes[2]):
        for jc in range(net.sizes[3]):
            if jx or jc:
                near.append(net.ident(net.shift((0, 0, jx, jc))))
    near = near + net.peers(extra)
    if experts:
        for jz in range(net.sizes[0]):
            for jy in range(net.sizes[1]):
                if jz or jy:
                    near.append(net.ident(net.shift((jz, jy, 0, 0))))
    for peer in near:
        pl.semaphore_signal(barrier, inc=1, device_id=peer, device_id_type=MESH)
    pl.semaphore_wait(barrier, len(near))


def merge_kernel(sizes, terms, out, landed, send, recv):
    net = Net(sizes)
    tensor_peers_enter(net, ())
    sent = scatter_tensor(net, terms, landed, send, recv)
    out[...] = scatter_finish(net, terms, landed, sent)


def merge_call(sizes, cid, terms):
    tensor = terms.shape[0]
    return pl.pallas_call(
        functools.partial(merge_kernel, sizes),
        out_shape=jax.ShapeDtypeStruct(terms.shape[1:], jnp.float32),
        in_specs=vmem(1),
        out_specs=pl.BlockSpec(memory_space=pltpu.VMEM),
        scratch_shapes=[
            pltpu.VMEM((tensor - 1,) + terms.shape[1:], terms.dtype),
            pltpu.SemaphoreType.DMA((tensor - 1,)),
            pltpu.SemaphoreType.DMA((tensor - 1,)),
        ],
        compiler_params=params(cid),
    )(terms)


def fold(net, part, out, core_in, core_sum, mid_in, mid_sum, low_in, low_sum, z_in, sems, x_first):
    z, y, x, c = net.at
    depth = net.sizes[0]
    kind = part.dtype
    wide = jnp.float32
    core_peer = net.peers([3])[0]
    first_dim, second_dim = (2, 1) if x_first else (1, 2)
    mid_peer, low_peer = net.peers([first_dim])[0], net.peers([second_dim])[0]
    first_at, second_at = net.at[first_dim], net.at[second_dim]

    def remote(source, target, stage, index, landing, peer):
        return pltpu.make_async_remote_copy(
            src_ref=source,
            dst_ref=target,
            send_sem=sems.at[stage, 0, index],
            recv_sem=sems.at[stage, 1, landing],
            device_id=peer,
            device_id_type=MESH,
        )

    zs = [(z + 1 + k) % depth if k < depth - 1 else z for k in range(depth)]
    core, mid, low, far = [], [], [], []
    for k in range(depth):
        copy = remote(part.at[zs[k], :, :, 1 - c], core_in.at[k], 0, k, k, core_peer)
        copy.start()
        core.append(copy)
    yield
    for k in range(depth):
        core[k].wait_recv()
        core_sum[k] = (part[zs[k], :, :, c].astype(wide) + core_in[k].astype(wide)).astype(kind)
        away = core_sum.at[k, :, 1 - first_at] if x_first else core_sum.at[k, 1 - first_at]
        copy = remote(away, mid_in.at[k], 1, k, k, mid_peer)
        copy.start()
        mid.append(copy)
        yield
    for lead in range(depth + 1):
        if lead < depth:
            k = lead
            mid[k].wait_recv()
            near = core_sum[k, :, first_at] if x_first else core_sum[k, first_at]
            mid_sum[k] = (near.astype(wide) + mid_in[k].astype(wide)).astype(kind)
            copy = remote(mid_sum.at[k, 1 - second_at], low_in.at[k], 2, k, k, low_peer)
            copy.start()
            low.append(copy)
            yield
        if lead > 0:
            k = lead - 1
            low[k].wait_recv()
            total = mid_sum[k, second_at].astype(wide) + low_in[k].astype(wide)
            if k == depth - 1:
                out[...] = total
            else:
                low_sum[k] = total.astype(kind)
                landing = depth - k - 2
                peer = net.ident([zs[k], y, x, c])
                copy = remote(low_sum.at[k], z_in.at[landing], 3, k, landing, peer)
                copy.start()
                far.append(copy)
            yield
    yield
    for k in range(depth - 1):
        far[k].wait_recv()
    total = out[...]
    for k in range(depth - 1):
        total = total + z_in[k].astype(wide)
    out[...] = total
    for copy in core + mid + low + far:
        copy.wait_send()


def fold_scratch(sizes, shape, kind):
    depth, ys, xs, cs = sizes
    return [
        pltpu.VMEM((depth, ys, xs) + shape, kind),
        pltpu.VMEM((depth, ys, xs) + shape, kind),
        pltpu.VMEM((depth, 2) + shape, kind),
        pltpu.VMEM((depth, 2) + shape, kind),
        pltpu.VMEM((depth,) + shape, kind),
        pltpu.VMEM((depth - 1,) + shape, kind),
        pltpu.VMEM((depth - 1,) + shape, kind),
        pltpu.SemaphoreType.DMA((4, 2, depth)),
    ]


def fold_kernel(sizes, firsts, *refs):
    n = len(firsts)
    net = Net(sizes)
    net.enter((0, 1, 2, 3))
    ins, outs, rest = refs[:n], refs[n : 2 * n], refs[2 * n :]
    together(
        [
            fold(net, ins[i], outs[i], *rest[8 * i : 8 * i + 8], firsts[i])
            for i in range(n)
        ]
    )


def fold_call(sizes, cid, arrays, firsts):
    shaped = [a.reshape(tuple(sizes) + a.shape[1:]) for a in arrays]
    scratch = []
    for a in arrays:
        scratch += fold_scratch(sizes, a.shape[1:], a.dtype)
    return pl.pallas_call(
        functools.partial(fold_kernel, sizes, firsts),
        out_shape=[jax.ShapeDtypeStruct(a.shape[1:], jnp.float32) for a in arrays],
        in_specs=vmem(len(arrays)),
        out_specs=vmem(len(arrays)),
        scratch_shapes=scratch,
        compiler_params=params(cid),
    )(*shaped)


def ring(net, part, y_in, y_sum, z_in, total, own, out, sems, send, recv):
    z, y, x, c = net.at
    depth = net.sizes[0]
    kind = part.dtype
    wide = jnp.float32
    y_peer = net.peers([1])[0]
    zs = [(z + 1 + k) % depth if k < depth - 1 else z for k in range(depth)]
    near, far = [], []

    def remote(source, target, stage, index, landing, peer):
        return pltpu.make_async_remote_copy(
            src_ref=source,
            dst_ref=target,
            send_sem=sems.at[stage, 0, index],
            recv_sem=sems.at[stage, 1, landing],
            device_id=peer,
            device_id_type=MESH,
        )

    for k in range(depth):
        copy = remote(part.at[zs[k], 1 - y], y_in.at[k], 0, k, k, y_peer)
        copy.start()
        near.append(copy)
    yield
    for k in range(depth):
        near[k].wait_recv()
        here = part[zs[k], y].astype(wide) + y_in[k].astype(wide)
        if k == depth - 1:
            total[...] = here
        else:
            y_sum[k] = here.astype(kind)
            landing = depth - k - 2
            peer = net.ident([zs[k], y, x, c])
            copy = remote(y_sum.at[k], z_in.at[landing], 1, k, landing, peer)
            copy.start()
            far.append(copy)
    yield
    for k in range(depth - 1):
        far[k].wait_recv()
    done = total[...]
    for k in range(depth - 1):
        done = done + z_in[k].astype(wide)
    own[...] = done.astype(kind)
    yield
    yield from spread(net, own, out, send, recv, (0, 1))
    for copy in near + far:
        copy.wait_send()


def ring_scratch(sizes, shape, kind):
    depth = sizes[0]
    count = depth * sizes[1]
    return [
        pltpu.VMEM((depth,) + shape, kind),
        pltpu.VMEM((depth - 1,) + shape, kind),
        pltpu.VMEM((depth - 1,) + shape, kind),
        pltpu.VMEM(shape, jnp.float32),
        pltpu.VMEM(shape, kind),
        pltpu.SemaphoreType.DMA((2, 2, depth)),
        pltpu.SemaphoreType.DMA((count - 1,)),
        pltpu.SemaphoreType.DMA((count,)),
    ]


def tail_kernel(sizes, gain_row, *refs):
    terms, d_middle, normed, inverse, gain, small, proj, merge = refs[:8]
    grad_all, proj_all, merge_all, small_out = refs[8:12]
    rest = refs[12:]
    landed, grad_own, small_in, small_sum, sc_send, sc_recv, g_send, g_recv, s_send, s_recv = rest[
        :10
    ]
    ring_one, ring_two = rest[10:18], rest[18:26]
    net = Net(sizes)
    tensor_peers_enter(net, (), True)
    sent = scatter_tensor(net, terms, landed, sc_send, sc_recv)
    rings = [
        ring(net, proj, *ring_one[:5], proj_all, *ring_one[5:]),
        ring(net, merge, *ring_two[:5], merge_all, *ring_two[5:]),
    ]
    for step in rings:
        next(step)
    for step in rings:
        next(step)
    d_first = scatter_finish(net, terms, landed, sent)
    scaled = d_first * gain[...]
    plain = normed[...]
    mean = jnp.mean(scaled, axis=-1, keepdims=True)
    mixed = jnp.mean(scaled * plain, axis=-1, keepdims=True)
    grad = d_middle[...] + inverse[...] * (scaled - mean - plain * mixed)
    grad_own[...] = grad.astype(jnp.bfloat16)
    part = jnp.sum(d_first * plain, axis=0, keepdims=True)
    row = lax.broadcasted_iota(jnp.int32, small.shape, 0)
    small_sum[0] = jnp.where(row == gain_row, part, small[...])
    copies = []

    def exchange(stage, slot, landing, place):
        copy = pltpu.make_async_remote_copy(
            src_ref=small_sum.at[stage],
            dst_ref=small_in.at[landing],
            send_sem=s_send.at[slot],
            recv_sem=s_recv.at[landing],
            device_id=net.ident(place),
            device_id_type=MESH,
        )
        copy.start()
        copies.append(copy)
        return copy

    exchange(0, 0, 0, net.shift((0, 0, 0, 1))).wait_recv()
    small_sum[1] = small_sum[0] + small_in[0]
    exchange(1, 1, 1, net.shift((0, 0, 1, 0))).wait_recv()
    small_sum[2] = small_sum[1] + small_in[1]
    grad_step = spread(net, grad_own, grad_all, g_send, g_recv, (2, 3))
    next(grad_step)
    slot = 2
    final = []
    for jz in range(sizes[0]):
        for jy in range(sizes[1]):
            if jz or jy:
                landing = 1 + slot_of((-jz, -jy, 0, 0), sizes, (0, 1))
                final.append(exchange(2, slot, landing, net.shift((jz, jy, 0, 0))))
                slot += 1
    for step in rings:
        next(step)
    for step in rings:
        next(step)
    next(grad_step)
    for step in rings:
        next(step)
    for copy in final:
        copy.wait_recv()
    total = small_sum[2]
    for k in range(len(final)):
        total = total + small_in[2 + k]
    small_out[...] = total
    for copy in copies:
        copy.wait_send()
    together([grad_step] + rings)


def tail_call(sizes, cid, gain_row, terms, d_middle, normed, inverse, gain, small, proj, merge):
    experts_axis, tensor = sizes[0] * sizes[1], sizes[2] * sizes[3]
    steps = 1 + experts_axis
    dma = pltpu.SemaphoreType.DMA
    shape = d_middle.shape
    low = jnp.bfloat16
    split = tuple(sizes[:2])
    proj = proj.reshape(split + (proj.shape[0] // experts_axis,) + proj.shape[1:])
    merge = merge.reshape(split + (merge.shape[0] // experts_axis,) + merge.shape[1:])
    return pl.pallas_call(
        functools.partial(tail_kernel, sizes, gain_row),
        out_shape=[
            jax.ShapeDtypeStruct((tensor,) + shape, low),
            jax.ShapeDtypeStruct((experts_axis,) + proj.shape[2:], low),
            jax.ShapeDtypeStruct((experts_axis,) + merge.shape[2:], low),
            jax.ShapeDtypeStruct(small.shape, jnp.float32),
        ],
        in_specs=vmem(8),
        out_specs=vmem(4),
        scratch_shapes=[
            pltpu.VMEM((tensor - 1,) + shape, low),
            pltpu.VMEM(shape, low),
            pltpu.VMEM((steps,) + small.shape, jnp.float32),
            pltpu.VMEM((3,) + small.shape, jnp.float32),
            dma((tensor - 1,)),
            dma((tensor - 1,)),
            dma((tensor - 1,)),
            dma((tensor,)),
            dma((steps,)),
            dma((steps,)),
        ]
        + ring_scratch(sizes, proj.shape[2:], low)
        + ring_scratch(sizes, merge.shape[2:], low),
        compiler_params=params(cid),
    )(terms, d_middle, normed, inverse, gain, small, proj, merge)


def on_device_dense(
    sizes,
    block_input,
    attn_gain,
    attn_proj,
    attn_merge,
    mixer_gain,
    router_weight,
    expert_up,
    expert_down,
    routes,
    keep_mask,
    out_grad,
):
    experts_axis, tensor = sizes[0] * sizes[1], sizes[2] * sizes[3]
    experts = experts_axis // PAIR
    tokens = block_input.shape[0]
    rows = -(-(-(-tokens // tensor)) // 8) * 8
    padded = rows * tensor
    local_width = attn_proj.shape[2]
    heads_here = local_width // HEAD
    score_scale = HEAD ** (-0.5)
    start = lax.axis_index("tensor") * rows
    low = jnp.bfloat16
    wide = jnp.float32

    def fill(array):
        return jnp.pad(array, ((0, padded - tokens), (0, 0)))

    def quarter(array):
        return lax.dynamic_slice_in_dim(array, start, rows, axis=0)

    input_q = quarter(fill(block_input)).astype(wide)
    grad_q_low = quarter(fill(out_grad))
    grad_q = grad_q_low.astype(wide)
    route_q = quarter(fill(routes))
    keep_q = quarter(fill(keep_mask))

    normed_one, unused = norm_parts(block_input.astype(wide))
    first_in = (normed_one * attn_gain).astype(low)
    normed_q, inverse_q = norm_parts(input_q)
    proj = jnp.einsum("td,dce->tce", first_in, attn_proj, preferred_element_type=wide).astype(low)
    head_grid = proj.reshape(tokens, 3, heads_here, HEAD)
    queries, key_heads, value_heads = head_grid[:, 0], head_grid[:, 1], head_grid[:, 2]
    raw = jnp.einsum("qhe,khe->hqk", queries, key_heads, preferred_element_type=wide) * score_scale
    row_top = jnp.max(raw, axis=-1, keepdims=True)
    powers = jnp.exp(raw - row_top)
    probs_wide = powers / jnp.sum(powers, axis=-1, keepdims=True)
    probs_low = probs_wide.astype(low)
    heads_out = jnp.einsum("hqk,khe->qhe", probs_low, value_heads, preferred_element_type=wide)
    heads_out = heads_out.astype(low).reshape(tokens, local_width)
    merge_terms = jnp.dot(fill(heads_out), attn_merge, preferred_element_type=wide).astype(low)

    merged = merge_call(sizes, 1, merge_terms.reshape(tensor, rows, D))
    middle = input_q + merged
    normed_two, inverse_two = norm_parts(middle)
    second_q = (normed_two * mixer_gain).astype(low)

    codes = jnp.concatenate([route_q, keep_q], axis=1).astype(wide).T
    codes = jnp.pad(codes, ((0, 4), (0, -rows % 128)))
    everywhere = (0, 1, 2, 3)
    second_all, grad_all, codes_all = gather_call(
        sizes,
        2,
        [second_q, grad_q_low, codes],
        [everywhere, (0, 2, 1, 3), everywhere],
    )
    total = experts_axis * padded
    arrived = second_all.reshape(total, D)
    grads = grad_all.reshape(total, D)

    label = lax.axis_index("expert") // PAIR
    code = codes_all[:, :4, :rows].transpose(0, 2, 1).reshape(total, 4)
    labels = jnp.arange(experts, dtype=wide)
    pick_all = (code[:, 0:1] == labels).astype(wide) - (code[:, 1:2] == labels).astype(wide)
    logits_all = jnp.dot(arrived, router_weight, preferred_element_type=wide)
    gate_all = jax.nn.sigmoid(jnp.sum(logits_all * pick_all, axis=1, keepdims=True))
    live_first = jnp.where(code[:, 0:1] == label.astype(wide), code[:, 2:3], 0.0)
    live_second = jnp.where(code[:, 1:2] == label.astype(wide), code[:, 3:4], 0.0)
    weight = live_first * gate_all + live_second * (1.0 - gate_all)
    side = live_first - live_second

    up, down = expert_up[0], expert_down[0]
    pre_act = jnp.dot(arrived, up, preferred_element_type=wide)
    hidden = gelu_value(pre_act).astype(low)
    partial_terms = jnp.dot(hidden, down, preferred_element_type=wide)
    moe_terms = (weight * partial_terms).astype(low)
    dots = jnp.sum(
        (partial_terms * grads.astype(wide)).reshape(experts_axis * tensor, rows, D), axis=2
    ) * side.reshape(experts_axis * tensor, rows)
    dots = jnp.broadcast_to(
        jnp.pad(dots, ((0, 0), (0, -rows % 128)))[:, None, :],
        (experts_axis * tensor, 8, -(-rows // 128) * 128),
    )
    d_rows = (weight * grads.astype(wide)).astype(low)
    d_hidden = lax.dot_general(d_rows, down, (((1,), (1,)), ((), ())), preferred_element_type=wide)
    down_local = lax.dot_general(
        hidden, d_rows, (((0,), (0,)), ((), ())), preferred_element_type=wide
    )
    d_pre = (d_hidden * gelu_slope(pre_act)).astype(low)
    up_local = lax.dot_general(arrived, d_pre, (((0,), (0,)), ((), ())), preferred_element_type=wide)
    d_terms = lax.dot_general(
        d_pre, up, (((1,), (1,)), ((), ())), preferred_element_type=wide
    ).astype(low)

    shape = (experts_axis * tensor, rows, D)
    moe, d_moe, dots_sum = fold_call(
        sizes,
        3,
        [moe_terms.reshape(shape), d_terms.reshape(shape), dots],
        (True, False, True),
    )
    block_q = (middle + moe).astype(low)
    mine = jnp.arange(experts, dtype=jnp.int32)
    pick = (route_q[:, 0:1] == mine).astype(wide) - (route_q[:, 1:2] == mine).astype(wide)
    logits = jnp.dot(second_q, router_weight, preferred_element_type=wide)
    gate_first = jax.nn.sigmoid(jnp.sum(logits * pick, axis=1))
    d_diff = dots_sum[0, :rows] * gate_first * (1.0 - gate_first)
    d_logits = (d_diff[:, None] * pick).astype(low)
    router_part = lax.dot_general(
        d_logits, second_q, (((0,), (0,)), ((), ())), preferred_element_type=wide
    )
    d_second = d_moe + lax.dot_general(
        d_logits, router_weight, (((1,), (1,)), ((), ())), preferred_element_type=wide
    )
    mixer_part = jnp.sum(d_second * normed_two, axis=0, keepdims=True)
    d_middle = grad_q + norm_back(d_second, normed_two, inverse_two, mixer_gain)
    d_low_q = d_middle.astype(low)

    low_rows, block_rows = gather_call(sizes, 4, [d_low_q, block_q], [(2, 3), (2, 3)])
    d_low = low_rows.reshape(padded, D)[:tokens]
    block_output = block_rows.reshape(padded, D)[:tokens]

    d_heads = lax.dot_general(
        d_low, attn_merge, (((1,), (1,)), ((), ())), preferred_element_type=wide
    ).astype(low)
    d_grid = d_heads.reshape(tokens, heads_here, HEAD)
    out_grid = heads_out.reshape(tokens, heads_here, HEAD)
    delta = jnp.sum(d_grid.astype(wide) * out_grid.astype(wide), axis=2).T
    d_probs = jnp.einsum("qhe,khe->hqk", d_grid, value_heads, preferred_element_type=wide)
    d_raw = (probs_wide * (d_probs - delta[..., None]) * score_scale).astype(low)
    d_queries = jnp.einsum("hqk,khe->qhe", d_raw, key_heads, preferred_element_type=wide)
    d_keys = jnp.einsum("hqk,qhe->khe", d_raw, queries, preferred_element_type=wide)
    d_values = jnp.einsum("hqk,qhe->khe", probs_low, d_grid, preferred_element_type=wide)
    d_proj = jnp.concatenate(
        [part.astype(low).reshape(tokens, local_width) for part in (d_queries, d_keys, d_values)],
        axis=1,
    )
    flat_proj = attn_proj.reshape(D, 3 * local_width)
    first_terms = lax.dot_general(
        fill(d_proj), flat_proj, (((1,), (1,)), ((), ())), preferred_element_type=wide
    ).astype(low)
    small = jnp.concatenate([router_part, mixer_part], axis=0)
    small = jnp.pad(small, ((0, 1 + -(experts + 2) % 8), (0, 0)))
    proj_local = lax.dot_general(
        first_in, d_proj, (((0,), (0,)), ((), ())), preferred_element_type=wide
    ).astype(low)
    merge_local = lax.dot_general(
        heads_out, d_low, (((0,), (0,)), ((), ())), preferred_element_type=wide
    ).astype(low)
    grad_rows, proj_all, merge_all, small_all = tail_call(
        sizes,
        5,
        experts + 1,
        first_terms.reshape(tensor, rows, D),
        d_middle,
        normed_q,
        inverse_q,
        attn_gain[None, :],
        small,
        proj_local,
        merge_local,
    )
    input_grad = grad_rows.reshape(padded, D)[:tokens].astype(wide)
    proj_grad = proj_all.astype(wide).reshape(D, 3, local_width)
    merge_grad = merge_all.astype(wide).reshape(local_width, D)
    return (
        block_output,
        input_grad,
        small_all[experts + 1],
        proj_grad,
        merge_grad,
        small_all[experts],
        small_all[:experts].T,
        up_local[None],
        down_local[None],
    )


def program_of(mesh):
    experts_axis, tensor = mesh.shape["expert"], mesh.shape["tensor"]
    if tensor != 4 or experts_axis % 2 or experts_axis < 4:
        return on_device
    capacity = max(8, 4 * TOK_DEV // (experts_axis // PAIR) // 8 * 8)
    rows = -(-(-(-TOK_DEV // tensor)) // 8) * 8
    if 4 * rows * tensor > 5 * capacity:
        return on_device
    return functools.partial(on_device_dense, (experts_axis // 2, 2, tensor // 2, 2))


def solution(mesh):
    in_specs = (
        P("expert", None),
        P(),
        P(None, None, "tensor"),
        P("tensor", None),
        P(),
        P(),
        P("expert", None, "tensor"),
        P("expert", "tensor", None),
        P("expert", None),
        P("expert", None),
        P("expert", None),
    )
    out_specs = (
        P("expert", None),
        P("expert", None),
        P(),
        P(None, None, "tensor"),
        P("tensor", None),
        P(),
        P(),
        P("expert", None, "tensor"),
        P("expert", "tensor", None),
    )
    return jax.shard_map(
        program_of(mesh), mesh=mesh, in_specs=in_specs, out_specs=out_specs, check_vma=False
    )
```
